32 devices in a mesh: scen: 2 (over x), row: 4 (over y, core), col: 4 (over z).
Axes of the slice: x: 2, y: 2, z: 4, core: 2. Of those that a mesh axis runs over, the one named last changes fastest.
Arguments:
- root_matrix: float32 [8192, 8192], P(('scen', 'row'), 'col'), may hold values from -1 to 32, as said below
- inverse_block: bfloat16 [32, 1024, 1024], P(('scen', 'row', 'col')), may hold values from -0.05 to 3, as said below
- link_tiles: bfloat16 [32, 20, 1024, 128], P(('scen', 'row', 'col')), may hold values from -0.1875 to 0.1875
- tile_mask: int32 [32, 64], P(('scen', 'row', 'col')), may hold values from 0 to 1, as said below
- panel_index: int32 [1], replicated, may hold values from 0 to 31
Outputs:
- trailing: float32 [8192, 8192], P(('scen', 'row'), 'col')
- factor: float32 [8192, 128], P(('scen', 'row', 'col'))
The draws below stay inside these ranges and needn't reach their ends.
Inputs may be any that keep to these rules, and one draw needn't show every extreme that they name: `root_matrix`: Symmetric, with the diagonal between 8 and 32 and every other entry of magnitude under 1. `inverse_block`: each block is symmetric positive definite, its diagonal between 1 and 3. `tile_mask`: each scenario flags between 4 and 20 tiles, at most 4 among each aligned group of 8 tiles (tiles 0 to 7, and so on); some scenario flags exactly 20 tiles, 4 in each of its first groups.
All inputs are finite; a program needn't handle non-finite values.
Results may differ from the reference program's by a relative error of at most 0.00049.
Values may be sent and summed in bfloat16 or wider, within the bound.
A program may use at most 64 MiB of HBM per device.

```python
import math
import jax
import jax.numpy as jnp
from jax import lax

NS = 1024
NF = 8192
PANEL = 128
TILE = 128
MAXT = 20
TGROUP = 8
TCAP = 4
NT = 64
SCENS = 32


def draw_root_matrix(key, part):
    noise_key, diag_key = jax.random.split(jax.random.fold_in(key, 11))
    noise_part = jnp.clip(0.1 * jax.random.normal(noise_key, (NF, NF), jnp.float32), -0.6, 0.6)
    symmetric = (noise_part + noise_part.T) * 0.7071
    diag_vals = jnp.exp(jax.random.uniform(diag_key, (NF,), jnp.float32, math.log(8.0), math.log(32.0)))
    row_ids = lax.broadcasted_iota(jnp.int32, (NF, NF), 0)
    col_ids = lax.broadcasted_iota(jnp.int32, (NF, NF), 1)
    return jnp.where(row_ids == col_ids, diag_vals[:, None], symmetric)


def one_inverse(scen_key):
    noise_key, diag_key = jax.random.split(scen_key)
    noise_part = jnp.clip(0.01 * jax.random.normal(noise_key, (NS, NS), jnp.float32), -0.035, 0.035)
    symmetric = (noise_part + noise_part.T) * 0.7071
    diag_vals = jnp.exp(jax.random.uniform(diag_key, (NS,), jnp.float32, 0.0, math.log(3.0)))
    row_ids = lax.broadcasted_iota(jnp.int32, (NS, NS), 0)
    col_ids = lax.broadcasted_iota(jnp.int32, (NS, NS), 1)
    return jnp.where(row_ids == col_ids, diag_vals[:, None], symmetric).astype(jnp.bfloat16)


def draw_inverse_block(key, part):
    scen_keys = jax.random.split(jax.random.fold_in(key, 13), SCENS)
    return lax.map(one_inverse, scen_keys)


def group_ranks(group_key):
    return jnp.argsort(jax.random.permutation(group_key, TGROUP))


def one_mask(scen_key, count, forced_here):
    slot_key, tile_key = jax.random.split(scen_key)
    group_count = NT // TGROUP
    slot_total = group_count * TCAP
    slot_pos = jnp.argsort(jax.random.permutation(slot_key, slot_total))
    slot_pos = jnp.where(forced_here, jnp.arange(slot_total), slot_pos)
    chosen = (slot_pos < count).astype(jnp.int32)
    per_group = jnp.sum(chosen.reshape(group_count, TCAP), axis=1)
    ranks = jax.vmap(group_ranks)(jax.random.split(tile_key, group_count))
    return (ranks < per_group[:, None]).astype(jnp.int32).reshape(NT)


def draw_tile_mask(key, part):
    count_key, order_key, full_key = jax.random.split(jax.random.fold_in(key, 17), 3)
    counts = jax.random.randint(count_key, (SCENS,), 4, MAXT + 1)
    forced = jax.random.randint(full_key, (), 0, SCENS)
    forced_flags = jnp.arange(SCENS) == forced
    counts = jnp.where(forced_flags, MAXT, counts)
    return jax.vmap(one_mask)(jax.random.split(order_key, SCENS), counts, forced_flags)


def shard_levels(rng, dims, pieces, least, high):
    level, own = 1.0, jax.random.fold_in(rng, 6)
    for dim, shards_of in pieces:
        heights = jnp.exp(jax.random.uniform(jax.random.fold_in(own, dim), (shards_of,), jnp.float32, least / len(pieces), high / len(pieces)))
        level = level * jnp.repeat(heights, dims[dim] // shards_of).reshape([-1 if axis == dim else 1 for axis in range(len(dims))])
    return level


def gaussian(own_key, shape, width, reach, pieces=(), held_as=jnp.bfloat16):
    entries = width * jax.random.normal(own_key, shape, jnp.float32)
    if pieces:
        entries = entries * shard_levels(own_key, shape, pieces, -0.22, 0.18)
    return jnp.clip(entries, -reach, reach).astype(held_as)


def setup_inputs(seed: int = 0) -> dict:
    key_list = jax.random.split(jax.random.key(seed), 6)
    return {
        "root_matrix": draw_root_matrix(jax.random.fold_in(key_list[5], 71), 0),
        "inverse_block": draw_inverse_block(jax.random.fold_in(key_list[5], 71), 0),
        "link_tiles": gaussian(key_list[2], (SCENS, MAXT, NS, TILE), NS ** -0.5, 0.1875, ((0, 32),)),
        "tile_mask": draw_tile_mask(jax.random.fold_in(key_list[5], 71), 0),
        "panel_index": jax.random.randint(key_list[4], (1,), 0, NF // (2 * PANEL)).astype(jnp.int32),
    }


def select_matrix(tile_flags, slot_count):
    slot_order = jnp.cumsum(tile_flags) - 1
    slot_ids = lax.broadcasted_iota(jnp.int32, (slot_count, tile_flags.shape[0]), 0)
    hit = (slot_order[None, :] == slot_ids) & (tile_flags[None, :] == 1)
    return jnp.where(hit, jnp.float32(1.0), jnp.float32(0.0))

def scenario_term(inverse, tiles_here, tile_flags, panel_at):
    slot_count, inner_rows, tile_rows = tiles_here.shape
    selector = select_matrix(tile_flags, slot_count)
    per_panel = PANEL // tile_rows
    picked = lax.dynamic_slice_in_dim(selector, panel_at * per_panel, per_panel, 1)
    columns = jnp.einsum('kj,knt->njt', picked, tiles_here.astype(jnp.float32), precision=lax.Precision.HIGHEST)
    columns = columns.reshape(inner_rows, PANEL).astype(jnp.bfloat16)
    weighted = jnp.dot(inverse.astype(jnp.float32), columns.astype(jnp.float32), preferred_element_type=jnp.float32).astype(jnp.bfloat16)
    product = jnp.einsum('knt,na->kta', tiles_here.astype(jnp.float32), weighted.astype(jnp.float32), precision=lax.Precision.HIGHEST)
    spread = jnp.einsum('kr,kta->rta', selector, product, precision=lax.Precision.HIGHEST)
    return spread.reshape(selector.shape[1] * tile_rows, PANEL)

def reference(root_matrix, inverse_block, link_tiles, tile_mask, panel_index):
    panel_at = panel_index[0]
    first_col = panel_at * PANEL
    base_cols = lax.dynamic_slice_in_dim(root_matrix, first_col, PANEL, 1)

    def accumulate(running, scenario_items):
        inverse, tiles_here, tile_flags = scenario_items
        return (running + scenario_term(inverse, tiles_here, tile_flags, panel_at), None)
    panel_sum, _ = lax.scan(accumulate, base_cols, (inverse_block, link_tiles, tile_mask))
    diagonal = lax.dynamic_slice_in_dim(panel_sum, first_col, PANEL, 0)
    chol_lower = jnp.linalg.cholesky(diagonal)
    solved = jax.scipy.linalg.solve_triangular(chol_lower, panel_sum.T, lower=True).T
    row_ids = lax.broadcasted_iota(jnp.int32, (NF, 1), 0)
    factor = jnp.where(row_ids >= first_col, solved, jnp.zeros_like(solved))
    rounded = factor.astype(jnp.bfloat16)
    ending = jnp.where(row_ids >= first_col + PANEL, rounded, jnp.zeros_like(rounded))
    update = jnp.dot(ending.astype(jnp.float32), ending.T.astype(jnp.float32), preferred_element_type=jnp.float32)
    return (root_matrix - update, factor)
```

```python
import jax
import jax.numpy as jnp
from jax import lax
from jax.experimental import pallas as pl
from jax.experimental.pallas import tpu as pltpu
from jax.sharding import PartitionSpec as P

PANEL = 128


def broadcast(block, axis, source):
    block = jnp.where(lax.axis_index(axis) == source, block, jnp.zeros_like(block))
    return lax.psum(block, axis)


def select_matrix(tile_flags, slot_count):
    tile_ids = jnp.arange(tile_flags.shape[0])
    slot_order = jnp.sum(jnp.where(tile_ids[None, :] <= tile_ids[:, None], tile_flags[None, :], 0), axis=1) - 1
    slot_ids = lax.broadcasted_iota(jnp.int32, (slot_count, tile_flags.shape[0]), 0)
    hit = (slot_order[None, :] == slot_ids) & (tile_flags[None, :] == 1)
    return jnp.where(hit, jnp.float32(1.0), jnp.float32(0.0))


def compact_term(inverse, tiles_here, tile_flags, panel_at):
    slot_count, inner_rows, tile_rows = tiles_here.shape
    selector = select_matrix(tile_flags, slot_count)
    per_panel = PANEL // tile_rows
    picked = lax.dynamic_slice_in_dim(selector, panel_at * per_panel, per_panel, 1)
    columns = jnp.einsum(
        "kj,knt->njt", picked.astype(jnp.bfloat16), tiles_here, preferred_element_type=jnp.float32
    )
    columns = columns.reshape(inner_rows, PANEL).astype(jnp.bfloat16)
    weighted = jnp.dot(inverse, columns, preferred_element_type=jnp.float32).astype(jnp.bfloat16)
    product = jnp.einsum("knt,na->kta", tiles_here, weighted, preferred_element_type=jnp.float32)
    return (selector, product)


def dense_term(selector, product, base_cols, base_start):
    spread = jnp.einsum("kr,kta->rta", selector, product, precision=lax.Precision.HIGHEST)
    scenario = spread.reshape(selector.shape[1] * product.shape[1], PANEL)
    own_block = lax.dynamic_slice_in_dim(scenario, base_start, base_cols.shape[0], 0) + base_cols
    return lax.dynamic_update_slice_in_dim(scenario, own_block, base_start, 0)


def lower_rows(diagonal, rows_here, first_row, first_col):
    chol_lower = jnp.linalg.cholesky(diagonal)
    solved = jax.scipy.linalg.solve_triangular(chol_lower, rows_here.T, lower=True).T
    row_ids = first_row + lax.broadcasted_iota(jnp.int32, (rows_here.shape[0], 1), 0)
    return jnp.where(row_ids >= first_col, solved, 0.0)


def trailing_rows(factor_part, first_row, first_col):
    rounded = factor_part.astype(jnp.bfloat16)
    row_ids = first_row + lax.broadcasted_iota(jnp.int32, (factor_part.shape[0], 1), 0)
    return jnp.where(row_ids >= first_col + PANEL, rounded, jnp.zeros_like(rounded))


def local(root_matrix, inverse_block, link_tiles, tile_mask, panel_index):
    panel_at = panel_index[0]
    tile_flags = tile_mask[0]
    selector, product = compact_term(inverse_block[0], link_tiles[0], tile_flags, panel_at)
    tile_count = selector.shape[1]
    tile_rows = product.shape[1]
    total_rows = tile_count * tile_rows
    row_block, col_block = root_matrix.shape
    scen_at = lax.axis_index("scen")
    row_at = lax.axis_index("row")
    col_at = lax.axis_index("col")
    row_count = lax.axis_size("row")
    col_count = lax.axis_size("col")
    scen_count = lax.axis_size("scen")
    block_at = scen_at * row_count + row_at
    first_col = panel_at * PANEL
    owner_col = first_col // col_block
    base_cols = lax.dynamic_slice_in_dim(root_matrix, first_col - owner_col * col_block, PANEL, 1)
    base_cols = jnp.where(col_at == owner_col, base_cols, 0.0)
    piece_rows = row_block // col_count
    scenario = dense_term(selector, product, base_cols, block_at * row_block)
    slab_rows = total_rows // scen_count
    slab_sum = lax.psum_scatter(scenario, "scen", scatter_dimension=0, tiled=True)
    slab_sum = lax.psum(slab_sum, ("row", "col"))
    owner_slab = first_col // slab_rows
    diag_part = lax.dynamic_slice_in_dim(slab_sum, first_col - owner_slab * slab_rows, PANEL, 0)
    diagonal = broadcast(diag_part, "scen", owner_slab)
    slab_first = scen_at * slab_rows
    slab_factor = lower_rows(diagonal, slab_sum, slab_first, first_col)
    factor_rows = lax.dynamic_slice_in_dim(
        slab_factor, (row_at * col_count + col_at) * piece_rows, piece_rows, 0
    )
    ending = trailing_rows(slab_factor, slab_first, first_col)
    all_factor = lax.all_gather(ending, "scen", axis=0, tiled=True)
    own_rows = lax.dynamic_slice_in_dim(all_factor, block_at * row_block, row_block, 0)
    own_cols = lax.dynamic_slice_in_dim(all_factor, col_at * col_block, col_block, 0)
    update = lax.dot_general(
        own_rows, own_cols, (((1,), (1,)), ((), ())), preferred_element_type=jnp.float32
    )
    return (root_matrix - update, factor_rows)


MESH_ID = pl.DeviceIdType.MESH
F32 = jnp.float32
BF16 = jnp.bfloat16


def term_kernel(panel_ref, mask_ref, inv_hbm, tiles_hbm, root_hbm, out_ref, diag_ref, inv, tiles, left, base, sems):
    slots = tiles.shape[0]
    f = panel_ref[0]
    scen_at, row_at, col_at = (lax.axis_index(a) for a in ("scen", "row", "col"))
    group = scen_at * lax.axis_size("row") + row_at
    tile_total = mask_ref.shape[1]
    wide = root_hbm.shape[1] // PANEL
    owner = col_at == f // wide

    def tile_copy(k):
        return pltpu.make_async_copy(tiles_hbm.at[k], tiles.at[k], sems.at[k])

    before = lax.fori_loop(0, f, lambda t, n: n + mask_ref[0, t], 0)
    linked = mask_ref[0, f]
    first = jnp.minimum(before, slots - 1)
    panel_copy = pltpu.make_async_copy(tiles_hbm.at[first], left, sems.at[slots + 1])
    panel_copy.start()
    inv_copy = pltpu.make_async_copy(inv_hbm, inv, sems.at[slots])
    inv_copy.start()
    total = lax.fori_loop(f, tile_total, lambda t, n: n + mask_ref[0, t], before)

    @pl.loop(0, total)
    def _(k):
        tile_copy(k).start()

    base_copy = pltpu.make_async_copy(
        root_hbm.at[:, pl.ds(pl.multiple_of(lax.rem(f, wide) * PANEL, PANEL), PANEL)], base, sems.at[slots + 2]
    )

    @pl.when(owner)
    def _():
        base_copy.start()

    panel_copy.wait()
    columns = jnp.where(linked == 1, left[...], jnp.zeros_like(left))
    inv_copy.wait()
    weighted = lax.dot_general(
        columns, inv[...], (((0,), (0,)), ((), ())), preferred_element_type=F32
    ).astype(BF16)

    def one(t, at):
        flag = mask_ref[0, t]

        @pl.when(flag == 1)
        def _():
            tile_copy(at).wait()
            out_ref[t] = jnp.dot(weighted, tiles[at], preferred_element_type=F32)

        @pl.when(flag != 1)
        def _():
            out_ref[t] = jnp.zeros(out_ref.shape[1:], F32)

        return at + flag

    lax.fori_loop(0, tile_total, one, 0)
    own_tiles = base.shape[0] // PANEL

    @pl.when(owner)
    def _():
        base_copy.wait()
        for i in range(own_tiles):
            at = group * own_tiles + i
            out_ref[at] = out_ref[at] + base[i * PANEL : (i + 1) * PANEL, :].T

    diag_ref[...] = out_ref[f]


def scenario_tiles(root_matrix, inverse, tiles, tile_mask, panel_index):
    slots, inner, tile_rows = tiles.shape
    tile_total = tile_mask.shape[1]
    smem = pl.BlockSpec(memory_space=pltpu.SMEM)
    hbm = pl.BlockSpec(memory_space=pltpu.HBM)
    vmem = pl.BlockSpec(memory_space=pltpu.VMEM)
    return pl.pallas_call(
        term_kernel,
        out_shape=(pltpu.VMEM((tile_total, PANEL, tile_rows), F32), pltpu.VMEM((PANEL, PANEL), F32)),
        in_specs=[smem, smem, hbm, hbm, hbm],
        out_specs=(vmem, vmem),
        scratch_shapes=[
            pltpu.VMEM(inverse.shape, BF16),
            pltpu.VMEM(tiles.shape, BF16),
            pltpu.VMEM((inner, tile_rows), BF16),
            pltpu.VMEM((root_matrix.shape[0], PANEL), F32),
            pltpu.SemaphoreType.DMA((slots + 3,)),
        ],
        compiler_params=pltpu.CompilerParams(vmem_limit_bytes=58 * 2**20),
        name="scenario_tiles",
    )(panel_index, tile_mask, inverse, tiles, root_matrix)


def remote(src, dst, send, recv, device):
    return pltpu.make_async_remote_copy(
        src_ref=src, dst_ref=dst, send_sem=send, recv_sem=recv, device_id=device, device_id_type=MESH_ID
    )


def invert_blocks(state, inv_ref, start, stop):
    lane = lax.broadcasted_iota(jnp.int32, (8, PANEL), 1)
    sub = lax.broadcasted_iota(jnp.int32, (8, 1), 0)

    def block(b, carry):
        at = pl.ds(pl.multiple_of(b * 8, 8), 8)
        strip = state[at, :]
        for i in range(8):
            col = jnp.sum(jnp.where(lane == b * 8 + i, strip[:, :PANEL], 0.0), axis=1, keepdims=True)
            pivot = col[i : i + 1, :]
            inv = lax.rsqrt(pivot)
            inv = inv * (1.5 - 0.5 * pivot * inv * inv)
            row = strip[i : i + 1, :] * inv
            coef = jnp.where(sub > i, col * inv, 0.0)
            strip = jnp.where(sub == i, row, strip - coef * row)
        inv_ref[at, :] = strip[:, PANEL:]
        later = jnp.where(lane >= b * 8 + 8, strip[:, :PANEL], 0.0)
        state[...] = state[...] - lax.dot_general(
            later, strip, (((0,), (0,)), ((), ())), preferred_element_type=F32, precision=lax.Precision.HIGHEST
        )
        return carry

    lax.fori_loop(start, stop, block, 0)


def gather_phase(panel_ref, piece_ref, inv_ref, factor_ref, rows_ref, cols_ref, send_z, recv_z,
                 send_x, send_y, recv_p, send_c, recv_c):
    s, r, c = (lax.axis_index(a) for a in ("scen", "row", "col"))
    y, k = r // 2, lax.rem(r, 2)
    rows = factor_ref.shape[0]
    far_x = lax.rem(s + c // 2, 2)
    far_y = lax.rem(y + c, 2)
    source = jnp.logical_and(far_x == 0, far_y == 0)
    x_to = (1 - s, r, c)
    y_to = (s, 2 * (1 - y) + k, c)
    core = (s, 2 * y + 1 - k, c)

    def row_at(z):
        return rows_ref.at[pl.ds(pl.multiple_of(z * rows, rows), rows)]

    def col_at(kk, z):
        return cols_ref.at[pl.ds(pl.multiple_of((kk * 4 + z) * rows, rows), rows)]

    f = panel_ref[0]
    first = (s * 4 + r) * (4 * rows) + c * rows
    for i in range(2):
        part = lax.dot_general(
            piece_ref[i], inv_ref[...], (((0,), (1,)), ((), ())),
            preferred_element_type=F32, precision=lax.Precision.HIGHEST,
        )
        ids = first + i * PANEL + lax.broadcasted_iota(jnp.int32, part.shape, 0)
        factor_ref[i * PANEL : (i + 1) * PANEL, :] = jnp.where(ids >= f * PANEL, part, 0.0)
        ending = jnp.where(ids >= f * PANEL + PANEL, part, 0.0).astype(BF16)
        rows_ref[pl.ds(pl.multiple_of(c * rows + i * PANEL, PANEL), PANEL), :] = ending

    z_copies = []
    for o in range(1, 4):
        cp = remote(row_at(c), row_at(c), send_z.at[o - 1], recv_z.at[o - 1], (s, r, lax.rem(c + o, 4)))
        cp.start()
        z_copies.append(cp)

    def z_arrival(o):
        remote(row_at(lax.rem(c + 4 - o, 4)), row_at(lax.rem(c + 4 - o, 4)), send_z.at[o - 1], recv_z.at[o - 1], core).wait_recv()

    for o in range(4):
        z = lax.rem(c + 4 - o, 4)
        here = col_at(k, z)
        to_x = remote(here, here, send_x.at[o], recv_p.at[o], x_to)
        to_y = remote(here, here, send_y.at[o], recv_p.at[o], y_to)

        @pl.when(source)
        def _():
            if o:
                z_arrival(o)
            here[...] = row_at(z)[...]
            to_x.start()
            to_y.start()

        @pl.when(jnp.logical_not(source))
        def _():
            to_x.wait_recv()

        @pl.when(jnp.logical_and(far_x == 1, far_y == 0) if o < 2 else jnp.logical_and(far_x == 0, far_y == 1))
        def _():
            (to_y if o < 2 else to_x).start()

        remote(here, here, send_c.at[o], recv_c.at[o], core).start()

    @pl.when(jnp.logical_not(source))
    def _():
        for o in range(1, 4):
            z_arrival(o)

    for o in range(4):
        z = lax.rem(c + 4 - o, 4)
        there, here = col_at(1 - k, z), col_at(k, z)
        remote(there, there, send_c.at[o], recv_c.at[o], core).wait_recv()
        remote(here, here, send_c.at[o], recv_c.at[o], core).wait_send()
        to_x = remote(here, here, send_x.at[o], recv_p.at[o], x_to)
        to_y = remote(here, here, send_y.at[o], recv_p.at[o], y_to)

        @pl.when(source)
        def _():
            to_x.wait_send()
            to_y.wait_send()

        @pl.when(jnp.logical_and(far_x == 1, far_y == 0) if o < 2 else jnp.logical_and(far_x == 0, far_y == 1))
        def _():
            (to_y if o < 2 else to_x).wait_send()

    for cp in z_copies:
        cp.wait_send()


def panel_kernel(panel_ref, tiles_hbm, diag_in, root_hbm, factor_ref, rows_ref, cols_ref, root_ref, own, got0, got1, got2, onward, acc, got3, got4, final,
                 dsum, dgot, dpart, dparts, diag_ref, state, inv_ref, piece_ref, send, recv, local_sem, root_sem, dsend, drecv,
                 *gather_sems):
    s, r, c = (lax.axis_index(a) for a in ("scen", "row", "col"))
    y, k = r // 2, lax.rem(r, 2)
    core = (s, 2 * y + 1 - k, c)
    x_to = (1 - s, r, c)
    y_to = (s, 2 * (1 - y) + k, c)
    z1 = c + 1 - 2 * lax.rem(c, 2)
    z2 = lax.rem(c + 2, 4)
    me = s * 8 + y * 4 + c

    def chip(o):
        q = lax.rem(me + o, 16)
        return q, (q // 8, 2 * lax.rem(q // 4, 2) + k, lax.rem(q, 4))

    barrier = pltpu.get_barrier_semaphore()
    pl.semaphore_signal(barrier, inc=1, device_id=core, device_id_type=MESH_ID)
    for o in range(1, 16):
        pl.semaphore_signal(barrier, inc=1, device_id=chip(o)[1], device_id_type=MESH_ID)
    pl.semaphore_wait(barrier, 16)

    core_diag = remote(diag_in, dgot, dsend.at[0], drecv.at[0], core)
    core_diag.start()
    far = (1 - s) * 2 + 1 - y
    over_x = (1 - s) * 2 + y
    over_y = s * 2 + 1 - y
    here = s * 2 + y
    par = lax.rem(c, 2)
    hi = c // 2
    order = (far, over_x, over_y, here)
    core_copy = []
    loads = []
    for n, i in enumerate(order):
        theirs = pl.ds(pl.multiple_of((i * 2 + 1 - k) * 8, 8), 8)
        ours = pl.ds(pl.multiple_of((i * 2 + k) * 8, 8), 8)
        cp = remote(tiles_hbm.at[theirs], got0.at[n], send.at[n], recv.at[n], core)
        cp.start()
        core_copy.append(cp)
        ld = pltpu.make_async_copy(tiles_hbm.at[ours], own.at[n], local_sem.at[n])
        ld.start()
        loads.append(ld)
    root_copy = []
    for i in range(4):
        part = pl.ds(i * (root_ref.shape[0] // 4), root_ref.shape[0] // 4)
        cp = pltpu.make_async_copy(root_hbm.at[part], root_ref.at[part], root_sem.at[i])
        cp.start()
        root_copy.append(cp)
    core_diag.wait()
    dsum[...] = diag_in[...] + dgot[...]
    out1 = []
    for o in range(1, 16):
        q, dev = chip(o)
        cp = remote(dsum.at[pl.ds(pl.multiple_of(q * 8, 8), 8)], dparts.at[o], dsend.at[o], drecv.at[o], dev)
        cp.start()
        out1.append(cp)

    pair = (2 * (1 - par), 2 * par)

    def crossing(j, h, step):
        n = 0 if step == 0 else 1 + h
        at = 4 + (j * 2 + h) * 2 + step
        return remote(own.at[n, pl.ds(4 * h + pair[j], 2)], got1.at[h, j, step], send.at[at], recv.at[at], y_to if h else x_to)

    first = [[[crossing(j, h, step) for step in range(2)] for h in range(2)] for j in range(2)]

    def pair_sum(n):
        loads[n].wait()
        core_copy[n].wait_recv()
        own[n] = own[n] + got0[n]

    pair_sum(0)
    first[0][0][0].start()
    first[0][1][0].start()
    pair_sum(1)
    first[0][0][1].start()
    pair_sum(2)
    first[0][1][1].start()
    pair_sum(3)
    for cp in out1:
        cp.wait_recv()
    total = dsum[pl.ds(pl.multiple_of(me * 8, 8), 8), :]
    for o in range(1, 16):
        total = total + dparts[o]
    dpart[...] = total
    diag_ref[pl.ds(pl.multiple_of(me * 8, 8), 8), :] = total
    out2 = []
    for o in range(1, 16):
        q, dev = chip(o)
        cp = remote(dpart, diag_ref.at[pl.ds(pl.multiple_of(me * 8, 8), 8)], dsend.at[15 + o], drecv.at[15 + o], dev)
        cp.start()
        out2.append(cp)
    second = []
    for j in range(2):
        for h in range(2):
            first[j][h][0].wait_recv()
            onward[j, h] = own[2 - h, pl.ds(4 * h + pair[j], 2)] + got1[h, j, 0]
            at = 12 + j * 2 + h
            cp = remote(onward.at[j, h], got2.at[j, h], send.at[at], recv.at[at], x_to if h else y_to)
            cp.start()
            second.append(cp)
            if j == 0:
                first[1][h][0].start()
        if j == 0:
            for cp in out2:
                cp.wait_recv()
            full = diag_ref[...]
            state[:, :PANEL] = 0.5 * (full + full.T)
            state[:, PANEL:] = jnp.where(
                lax.broadcasted_iota(jnp.int32, (PANEL, PANEL), 0) == lax.broadcasted_iota(jnp.int32, (PANEL, PANEL), 1),
                1.0, 0.0,
            )
        invert_blocks(state, inv_ref, (0, 6)[j], (2, 9)[j])
        for h in range(2):
            first[j][h][1].wait_recv()
            acc[j, h] = own[3, pl.ds(4 * h + pair[j], 2)] + got1[h, j, 1]
            if j == 0:
                first[1][h][1].start()
        invert_blocks(state, inv_ref, (2, 9)[j], (4, 12)[j])
        for h in range(2):
            second[2 * j + h].wait_recv()
            acc[j, h] = acc[j, h] + got2[j, h]
        if j == 0:
            z_out = remote(acc.at[0], got3, send.at[16], recv.at[16], (s, r, z1))
            z_out.start()
            invert_blocks(state, inv_ref, 4, 6)
    z_out.wait_recv()
    final[...] = acc[1, 1 - hi] + got3[1 - hi]
    last = remote(final, got4, send.at[17], recv.at[17], (s, r, z2))
    last.start()
    mine = acc[1, hi] + got3[hi]
    invert_blocks(state, inv_ref, 12, 16)
    last.wait_recv()
    piece_ref[...] = mine + got4[...]
    for cp in core_copy + out1 + out2 + second + [z_out, last]:
        cp.wait_send()
    for j in range(2):
        for h in range(2):
            for step in range(2):
                first[j][h][step].wait_send()
    gather_phase(panel_ref, piece_ref, inv_ref, factor_ref, rows_ref, cols_ref, *gather_sems)
    for cp in root_copy:
        cp.wait()


def panel_factor(panel_index, tiles, diag, root_matrix):
    row_block, col_block = root_matrix.shape
    tile = tiles.shape[1:]
    vmem = pl.BlockSpec(memory_space=pltpu.VMEM)
    return pl.pallas_call(
        panel_kernel,
        out_shape=(
            pltpu.VMEM((2 * PANEL, PANEL), F32),
            pltpu.VMEM((row_block, PANEL), BF16),
            pltpu.VMEM((col_block, PANEL), BF16),
            pltpu.VMEM((row_block, col_block), F32),
        ),
        in_specs=[
            pl.BlockSpec(memory_space=pltpu.SMEM), vmem, vmem, pl.BlockSpec(memory_space=pltpu.HBM),
        ],
        out_specs=(vmem, vmem, vmem, vmem),
        scratch_shapes=[
            pltpu.VMEM((4, 8, *tile), F32),
            pltpu.VMEM((4, 8, *tile), F32),
            pltpu.VMEM((2, 2, 2, 2, *tile), F32),
            pltpu.VMEM((2, 2, 2, *tile), F32),
            pltpu.VMEM((2, 2, 2, *tile), F32),
            pltpu.VMEM((2, 2, 2, *tile), F32),
            pltpu.VMEM((2, 2, *tile), F32),
            pltpu.VMEM((2, *tile), F32),
            pltpu.VMEM((2, *tile), F32),
            pltpu.VMEM(tile, F32),
            pltpu.VMEM(tile, F32),
            pltpu.VMEM((8, PANEL), F32),
            pltpu.VMEM((16, 8, PANEL), F32),
            pltpu.VMEM(tile, F32),
            pltpu.VMEM((PANEL, 2 * PANEL), F32),
            pltpu.VMEM(tile, F32),
            pltpu.VMEM((2, *tile), F32),
            pltpu.SemaphoreType.DMA((18,)),
            pltpu.SemaphoreType.DMA((18,)),
            pltpu.SemaphoreType.DMA((4,)),
            pltpu.SemaphoreType.DMA((4,)),
            pltpu.SemaphoreType.DMA((31,)),
            pltpu.SemaphoreType.DMA((31,)),
            pltpu.SemaphoreType.DMA((3,)),
            pltpu.SemaphoreType.DMA((3,)),
            *[pltpu.SemaphoreType.DMA((4,))] * 5,
        ],
        compiler_params=pltpu.CompilerParams(collective_id=0, has_side_effects=True, vmem_limit_bytes=40 * 2**20),
        name="panel_factor",
    )(panel_index, tiles, diag, root_matrix)


def trailing_kernel(root_ref, rows_ref, cols_ref, factor_ref, out_hbm, factor_hbm, held, sems):
    count = held.shape[0]
    rows = held.shape[1]
    copies = [pltpu.make_async_copy(factor_ref, factor_hbm, sems.at[count])]
    copies[0].start()
    for i in range(count):
        part = pl.ds(i * rows, rows)
        held[i] = root_ref[part, :] - lax.dot_general(
            rows_ref[part, :], cols_ref[...], (((1,), (1,)), ((), ())), preferred_element_type=F32
        )
        cp = pltpu.make_async_copy(held.at[i], out_hbm.at[part], sems.at[i])
        cp.start()
        copies.append(cp)
    for cp in copies:
        cp.wait()


def trailing_update(root, rows, cols, factor):
    hbm = pl.BlockSpec(memory_space=pltpu.HBM)
    vmem = pl.BlockSpec(memory_space=pltpu.VMEM)
    chunks = 8
    return pl.pallas_call(
        trailing_kernel,
        out_shape=(
            jax.ShapeDtypeStruct(root.shape, F32),
            jax.ShapeDtypeStruct(factor.shape, F32),
        ),
        in_specs=[vmem] * 4,
        out_specs=(hbm, hbm),
        scratch_shapes=[
            pltpu.VMEM((chunks, root.shape[0] // chunks, root.shape[1]), F32),
            pltpu.SemaphoreType.DMA((chunks + 1,)),
        ],
        compiler_params=pltpu.CompilerParams(vmem_limit_bytes=40 * 2**20),
        name="trailing_update",
    )(root, rows, cols, factor)


def direct(root_matrix, inverse_block, link_tiles, tile_mask, panel_index):
    tiles, diag = scenario_tiles(root_matrix, inverse_block[0], link_tiles[0], tile_mask, panel_index)
    factor, rows, cols, root = panel_factor(panel_index, tiles, diag, root_matrix)
    return trailing_update(root, rows, cols, factor)


def solution(mesh):
    in_specs = (
        P(("scen", "row"), "col"),
        P(("scen", "row", "col"), None, None),
        P(("scen", "row", "col"), None, None, None),
        P(("scen", "row", "col"), None),
        P(),
    )
    out_specs = (P(("scen", "row"), "col"), P(("scen", "row", "col"), None))
    sizes = tuple(mesh.shape[a] for a in ("scen", "row", "col"))
    body = direct if sizes == (2, 4, 4) else local
    return jax.shard_map(body, mesh=mesh, in_specs=in_specs, out_specs=out_specs, check_vma=False)
```

```python
import jax
import jax.numpy as jnp
from jax import lax
from jax.experimental import pallas as pl
from jax.experimental.pallas import tpu as pltpu
from jax.sharding import PartitionSpec as P

PANEL = 128


def broadcast(block, axis, source):
    block = jnp.where(lax.axis_index(axis) == source, block, jnp.zeros_like(block))
    return lax.psum(block, axis)


def select_matrix(tile_flags, slot_count):
    tile_ids = jnp.arange(tile_flags.shape[0])
    slot_order = jnp.sum(jnp.where(tile_ids[None, :] <= tile_ids[:, None], tile_flags[None, :], 0), axis=1) - 1
    slot_ids = lax.broadcasted_iota(jnp.int32, (slot_count, tile_flags.shape[0]), 0)
    hit = (slot_order[None, :] == slot_ids) & (tile_flags[None, :] == 1)
    return jnp.where(hit, jnp.float32(1.0), jnp.float32(0.0))


def compact_term(inverse, tiles_here, tile_flags, panel_at):
    slot_count, inner_rows, tile_rows = tiles_here.shape
    selector = select_matrix(tile_flags, slot_count)
    per_panel = PANEL // tile_rows
    picked = lax.dynamic_slice_in_dim(selector, panel_at * per_panel, per_panel, 1)
    columns = jnp.einsum(
        "kj,knt->njt", picked.astype(jnp.bfloat16), tiles_here, preferred_element_type=jnp.float32
    )
    columns = columns.reshape(inner_rows, PANEL).astype(jnp.bfloat16)
    weighted = jnp.dot(inverse, columns, preferred_element_type=jnp.float32).astype(jnp.bfloat16)
    product = jnp.einsum("knt,na->kta", tiles_here, weighted, preferred_element_type=jnp.float32)
    return (selector, product)


def dense_term(selector, product, base_cols, base_start):
    spread = jnp.einsum("kr,kta->rta", selector, product, precision=lax.Precision.HIGHEST)
    scenario = spread.reshape(selector.shape[1] * product.shape[1], PANEL)
    own_block = lax.dynamic_slice_in_dim(scenario, base_start, base_cols.shape[0], 0) + base_cols
    return lax.dynamic_update_slice_in_dim(scenario, own_block, base_start, 0)


def lower_rows(diagonal, rows_here, first_row, first_col):
    chol_lower = jnp.linalg.cholesky(diagonal)
    solved = jax.scipy.linalg.solve_triangular(chol_lower, rows_here.T, lower=True).T
    row_ids = first_row + lax.broadcasted_iota(jnp.int32, (rows_here.shape[0], 1), 0)
    return jnp.where(row_ids >= first_col, solved, 0.0)


def trailing_rows(factor_part, first_row, first_col):
    rounded = factor_part.astype(jnp.bfloat16)
    row_ids = first_row + lax.broadcasted_iota(jnp.int32, (factor_part.shape[0], 1), 0)
    return jnp.where(row_ids >= first_col + PANEL, rounded, jnp.zeros_like(rounded))


def local(root_matrix, inverse_block, link_tiles, tile_mask, panel_index):
    panel_at = panel_index[0]
    tile_flags = tile_mask[0]
    selector, product = compact_term(inverse_block[0], link_tiles[0], tile_flags, panel_at)
    tile_count = selector.shape[1]
    tile_rows = product.shape[1]
    total_rows = tile_count * tile_rows
    row_block, col_block = root_matrix.shape
    scen_at = lax.axis_index("scen")
    row_at = lax.axis_index("row")
    col_at = lax.axis_index("col")
    row_count = lax.axis_size("row")
    col_count = lax.axis_size("col")
    scen_count = lax.axis_size("scen")
    block_at = scen_at * row_count + row_at
    first_col = panel_at * PANEL
    owner_col = first_col // col_block
    base_cols = lax.dynamic_slice_in_dim(root_matrix, first_col - owner_col * col_block, PANEL, 1)
    base_cols = jnp.where(col_at == owner_col, base_cols, 0.0)
    piece_rows = row_block // col_count
    scenario = dense_term(selector, product, base_cols, block_at * row_block)
    slab_rows = total_rows // scen_count
    slab_sum = lax.psum_scatter(scenario, "scen", scatter_dimension=0, tiled=True)
    slab_sum = lax.psum(slab_sum, ("row", "col"))
    owner_slab = first_col // slab_rows
    diag_part = lax.dynamic_slice_in_dim(slab_sum, first_col - owner_slab * slab_rows, PANEL, 0)
    diagonal = broadcast(diag_part, "scen", owner_slab)
    slab_first = scen_at * slab_rows
    slab_factor = lower_rows(diagonal, slab_sum, slab_first, first_col)
    factor_rows = lax.dynamic_slice_in_dim(
        slab_factor, (row_at * col_count + col_at) * piece_rows, piece_rows, 0
    )
    ending = trailing_rows(slab_factor, slab_first, first_col)
    all_factor = lax.all_gather(ending, "scen", axis=0, tiled=True)
    own_rows = lax.dynamic_slice_in_dim(all_factor, block_at * row_block, row_block, 0)
    own_cols = lax.dynamic_slice_in_dim(all_factor, col_at * col_block, col_block, 0)
    update = lax.dot_general(
        own_rows, own_cols, (((1,), (1,)), ((), ())), preferred_element_type=jnp.float32
    )
    return (root_matrix - update, factor_rows)


MESH_ID = pl.DeviceIdType.MESH
F32 = jnp.float32
BF16 = jnp.bfloat16


def term_kernel(panel_ref, mask_ref, inv_hbm, tiles_hbm, root_hbm, out_ref, diag_ref, inv, tiles, left, base, sems):
    slots = tiles.shape[0]
    f = panel_ref[0]
    scen_at, row_at, col_at = (lax.axis_index(a) for a in ("scen", "row", "col"))
    group = scen_at * lax.axis_size("row") + row_at
    tile_total = mask_ref.shape[1]
    wide = root_hbm.shape[1] // PANEL
    owner = col_at == f // wide

    def tile_copy(k):
        return pltpu.make_async_copy(tiles_hbm.at[k], tiles.at[k], sems.at[k])

    before = lax.fori_loop(0, f, lambda t, n: n + mask_ref[0, t], 0)
    linked = mask_ref[0, f]
    first = jnp.minimum(before, slots - 1)
    panel_copy = pltpu.make_async_copy(tiles_hbm.at[first], left, sems.at[slots + 1])
    panel_copy.start()
    inv_copy = pltpu.make_async_copy(inv_hbm, inv, sems.at[slots])
    inv_copy.start()
    total = lax.fori_loop(f, tile_total, lambda t, n: n + mask_ref[0, t], before)

    @pl.loop(0, total)
    def _(k):
        tile_copy(k).start()

    base_copy = pltpu.make_async_copy(
        root_hbm.at[:, pl.ds(pl.multiple_of(lax.rem(f, wide) * PANEL, PANEL), PANEL)], base, sems.at[slots + 2]
    )

    @pl.when(owner)
    def _():
        base_copy.start()

    panel_copy.wait()
    columns = jnp.where(linked == 1, left[...], jnp.zeros_like(left))
    inv_copy.wait()
    weighted = lax.dot_general(
        columns, inv[...], (((0,), (0,)), ((), ())), preferred_element_type=F32
    ).astype(BF16)

    def one(t, at):
        flag = mask_ref[0, t]

        @pl.when(flag == 1)
        def _():
            tile_copy(at).wait()
            out_ref[t] = jnp.dot(weighted, tiles[at], preferred_element_type=F32)

        @pl.when(flag != 1)
        def _():
            out_ref[t] = jnp.zeros(out_ref.shape[1:], F32)

        return at + flag

    lax.fori_loop(0, tile_total, one, 0)
    own_tiles = base.shape[0] // PANEL

    @pl.when(owner)
    def _():
        base_copy.wait()
        for i in range(own_tiles):
            at = group * own_tiles + i
            out_ref[at] = out_ref[at] + base[i * PANEL : (i + 1) * PANEL, :].T

    diag_ref[...] = out_ref[f]


def scenario_tiles(root_matrix, inverse, tiles, tile_mask, panel_index):
    slots, inner, tile_rows = tiles.shape
    tile_total = tile_mask.shape[1]
    smem = pl.BlockSpec(memory_space=pltpu.SMEM)
    hbm = pl.BlockSpec(memory_space=pltpu.HBM)
    vmem = pl.BlockSpec(memory_space=pltpu.VMEM)
    return pl.pallas_call(
        term_kernel,
        out_shape=(pltpu.VMEM((tile_total, PANEL, tile_rows), F32), pltpu.VMEM((PANEL, PANEL), F32)),
        in_specs=[smem, smem, hbm, hbm, hbm],
        out_specs=(vmem, vmem),
        scratch_shapes=[
            pltpu.VMEM(inverse.shape, BF16),
            pltpu.VMEM(tiles.shape, BF16),
            pltpu.VMEM((inner, tile_rows), BF16),
            pltpu.VMEM((root_matrix.shape[0], PANEL), F32),
            pltpu.SemaphoreType.DMA((slots + 3,)),
        ],
        compiler_params=pltpu.CompilerParams(vmem_limit_bytes=58 * 2**20),
        name="scenario_tiles",
    )(panel_index, tile_mask, inverse, tiles, root_matrix)


def remote(src, dst, send, recv, device):
    return pltpu.make_async_remote_copy(
        src_ref=src, dst_ref=dst, send_sem=send, recv_sem=recv, device_id=device, device_id_type=MESH_ID
    )


BLOCK = 16
CODED = 2 * PANEL + 16


def invert_blocks(state, inv_ref, start, stop):
    lane = lax.broadcasted_iota(jnp.int32, (BLOCK, PANEL), 1)
    sub = lax.broadcasted_iota(jnp.int32, (BLOCK, PANEL), 0)

    def block(b, carry):
        at = pl.ds(pl.multiple_of(b * BLOCK, BLOCK), BLOCK)
        left, right = state[at, :PANEL], state[at, PANEL:]
        cols = [
            jnp.broadcast_to(
                jnp.sum(jnp.where(lane == b * BLOCK + j, left, 0.0), axis=1, keepdims=True), (BLOCK, PANEL)
            )
            for j in range(BLOCK)
        ]
        for i in range(BLOCK):
            pivot = cols[i][i : i + 1, :]
            inv = lax.rsqrt(pivot)
            inv = inv * (1.5 - 0.5 * pivot * inv * inv)
            coef = jnp.where(sub > i, cols[i] * inv, 0.0)
            for j in range(i + 1, BLOCK):
                cols[j] = cols[j] - coef * (cols[j][i : i + 1, :] * inv)
            row_l, row_r = left[i : i + 1, :] * inv, right[i : i + 1, :] * inv
            left = jnp.where(sub == i, row_l, left - coef * row_l)
            right = jnp.where(sub == i, row_r, right - coef * row_r)
        inv_ref[at, :] = right
        later = jnp.where(lane >= b * BLOCK + BLOCK, left, 0.0)
        state[...] = state[...] - lax.dot_general(
            later, jnp.concatenate([left, right], axis=1), (((0,), (0,)), ((), ())),
            preferred_element_type=F32, precision=lax.Precision.HIGHEST,
        )
        return carry

    lax.fori_loop(start, stop, block, 0)


def code_scale(exponent):
    return jnp.exp2(15.0 - exponent) * 0.995


def encode(pair, out):
    exps = []
    for t in range(2):
        top = jnp.max(jnp.abs(pair[t]), axis=0, keepdims=True)
        exponent = jnp.ceil(jnp.log2(jnp.maximum(top, 1e-30)))
        out[t * PANEL : (t + 1) * PANEL, :] = jnp.round(pair[t] * code_scale(exponent)).astype(jnp.int32).astype(jnp.int16)
        exps.append(jnp.broadcast_to(exponent, (8, PANEL)))
    out[2 * PANEL : CODED, :] = jnp.concatenate(exps, axis=0).astype(jnp.int32).astype(jnp.int16)


def decode(coded):
    exponent = coded[2 * PANEL : CODED, :].astype(jnp.int32).astype(F32)
    return [
        coded[t * PANEL : (t + 1) * PANEL, :].astype(jnp.int32).astype(F32)
        * (1.0 / code_scale(exponent[8 * t : 8 * t + 1, :]))
        for t in range(2)
    ]


def gather_phase(rows_ref, cols_ref, send_z, recv_z, send_x, send_y, recv_p, send_c, recv_c):
    s, r, c = (lax.axis_index(a) for a in ("scen", "row", "col"))
    y, k = r // 2, lax.rem(r, 2)
    rows = 2 * PANEL
    far_x = lax.rem(s + c // 2, 2)
    far_y = lax.rem(y + c, 2)
    source = jnp.logical_and(far_x == 0, far_y == 0)
    x_to = (1 - s, r, c)
    y_to = (s, 2 * (1 - y) + k, c)
    z1 = (s, r, c + 1 - 2 * lax.rem(c, 2))
    core = (s, 2 * y + 1 - k, c)
    par = lax.rem(c, 2)
    pieces = (par, par + 2, 1 - par, 3 - par)

    def row_at(z):
        return rows_ref.at[pl.ds(pl.multiple_of(z * rows, rows), rows)]

    def col_at(kk, z):
        return cols_ref.at[pl.ds(pl.multiple_of((kk * 4 + z) * rows, rows), rows)]

    def z_copy(i):
        return remote(row_at(pieces[i]), row_at(pieces[i]), send_z.at[i], recv_z.at[i], z1)

    def z_arrival(i):
        return remote(row_at(pieces[2 + i]), row_at(pieces[2 + i]), send_z.at[i], recv_z.at[i], z1)

    def first_hop(o, to, sems):
        return remote(row_at(pieces[o]), col_at(k, pieces[o]), sems.at[o], recv_p.at[o], to)

    def onward(o):
        here = col_at(k, pieces[o])
        return remote(here, here, (send_x if o % 2 else send_y).at[o], recv_p.at[o], x_to if o % 2 else y_to)

    def forwards(o):
        if o % 2:
            return jnp.logical_and(far_x == 0, far_y == 1)
        return jnp.logical_and(far_x == 1, far_y == 0)

    def to_core(o, kk):
        here = col_at(kk, pieces[o])
        return remote(here, here, send_c.at[o], recv_c.at[o], core)

    @pl.when(source)
    def _():
        for o in range(2):
            first_hop(o, x_to, send_x).start()
            first_hop(o, y_to, send_y).start()

    for i in range(2):
        z_copy(i).start()

    for o in range(4):

        @pl.when(source)
        def _():
            if o >= 2:
                z_arrival(o - 2).wait_recv()
                first_hop(o, x_to, send_x).start()
                first_hop(o, y_to, send_y).start()
            col_at(k, pieces[o])[...] = row_at(pieces[o])[...]

        @pl.when(jnp.logical_not(source))
        def _():
            onward(o).wait_recv()

        @pl.when(forwards(o))
        def _():
            onward(o).start()

        to_core(o, k).start()

    @pl.when(jnp.logical_not(source))
    def _():
        for i in range(2):
            z_arrival(i).wait_recv()

    for o in range(4):
        to_core(o, 1 - k).wait_recv()
        to_core(o, k).wait_send()

        @pl.when(source)
        def _():
            first_hop(o, x_to, send_x).wait_send()
            first_hop(o, y_to, send_y).wait_send()

        @pl.when(forwards(o))
        def _():
            onward(o).wait_send()

    for i in range(2):
        z_copy(i).wait_send()


def panel_kernel(panel_ref, tiles_ref, diag_in, root_hbm, factor_ref, rows_ref, cols_ref, root_ref, got0, acc, coded, got,
                 dsum, dgot, dpart, dparts, diag_ref, state, inv_ref, core_send, core_recv, send, recv, root_sem,
                 dsend, drecv, *gather_sems):
    s, r, c = (lax.axis_index(a) for a in ("scen", "row", "col"))
    y, k = r // 2, lax.rem(r, 2)
    core = (s, 2 * y + 1 - k, c)
    x_to = (1 - s, r, c)
    y_to = (s, 2 * (1 - y) + k, c)
    par = lax.rem(c, 2)
    hi = c // 2
    z1 = (s, r, c + 1 - 2 * par)
    z2 = (s, r, lax.rem(c + 2, 4))
    me = s * 8 + y * 4 + c

    def chip(o):
        q = lax.rem(me + o, 16)
        return q, (q // 8, 2 * lax.rem(q // 4, 2) + k, lax.rem(q, 4))

    barrier = pltpu.get_barrier_semaphore()
    pl.semaphore_signal(barrier, inc=1, device_id=core, device_id_type=MESH_ID)
    for o in range(1, 16):
        pl.semaphore_signal(barrier, inc=1, device_id=chip(o)[1], device_id_type=MESH_ID)
    pl.semaphore_wait(barrier, 16)

    core_diag = remote(diag_in, dgot, dsend.at[0], drecv.at[0], core)
    core_diag.start()
    order = ((1 - s) * 2 + 1 - y, (1 - s) * 2 + y, s * 2 + 1 - y, s * 2 + y)
    core_copy = []
    for n, i in enumerate(order):
        theirs = pl.ds(pl.multiple_of((i * 2 + 1 - k) * 8, 8), 8)
        cp = remote(tiles_ref.at[theirs], got0.at[n], core_send.at[n], core_recv.at[n], core)
        cp.start()
        core_copy.append(cp)
    root_copy = []
    for i in range(4):
        part = pl.ds(i * (root_ref.shape[0] // 4), root_ref.shape[0] // 4)
        cp = pltpu.make_async_copy(root_hbm.at[part], root_ref.at[part], root_sem.at[i])
        cp.start()
        root_copy.append(cp)

    core_diag.wait()
    dsum[...] = diag_in[...] + dgot[...]
    out1 = []
    for o in range(1, 16):
        q, dev = chip(o)
        cp = remote(dsum.at[pl.ds(pl.multiple_of(q * 8, 8), 8)], dparts.at[o], dsend.at[o], drecv.at[o], dev)
        cp.start()
        out1.append(cp)

    pair = (2 * (1 - par), 2 * par)

    def core_sum(n, h, j):
        i = order[n]
        return [
            tiles_ref[(i * 2 + k) * 8 + 4 * h + pair[j] + t] + got0[n, 4 * h + pair[j] + t] for t in range(2)
        ]

    def plus(a, b):
        return [a[t] + b[t] for t in range(2)]

    def ship(at, value, to):
        encode(value, coded.at[at])
        cp = remote(coded.at[at], got.at[at], send.at[at], recv.at[at], to)
        return cp

    ways = (x_to, y_to)
    far, over, onward = ([[None, None], [None, None]] for _ in range(3))

    def far_send(j):
        for h in range(2):
            far[j][h] = ship(j * 2 + h, core_sum(0, h, j), ways[h])
            far[j][h].start()

    def over_make(j):
        for h in range(2):
            over[j][h] = ship(4 + j * 2 + h, core_sum(1 + h, h, j), ways[h])

    def onward_send(j):
        for h in range(2):
            far[j][h].wait_recv()
            value = plus(core_sum(2 - h, h, j), decode(got[j * 2 + h]))
            onward[j][h] = ship(8 + j * 2 + h, value, ways[1 - h])
            onward[j][h].start()

    def keep(j, h, value):
        for t in range(2):
            acc[j, h, t] = value[t]

    def kept(j, h):
        return [acc[j, h, t] for t in range(2)]

    core_copy[0].wait_recv()
    far_send(0)
    core_copy[1].wait_recv()
    core_copy[2].wait_recv()
    over_make(0)
    for h in range(2):
        over[0][h].start()
    far_send(1)
    over_make(1)
    for cp in out1:
        cp.wait_recv()
    total = dsum[pl.ds(pl.multiple_of(me * 8, 8), 8), :]
    for o in range(1, 16):
        total = total + dparts[o]
    dpart[...] = total
    diag_ref[pl.ds(pl.multiple_of(me * 8, 8), 8), :] = total
    out2 = []
    for o in range(1, 16):
        q, dev = chip(o)
        cp = remote(dpart, diag_ref.at[pl.ds(pl.multiple_of(me * 8, 8), 8)], dsend.at[15 + o], drecv.at[15 + o], dev)
        cp.start()
        out2.append(cp)
    onward_send(0)
    for h in range(2):
        over[1][h].start()
    core_copy[3].wait_recv()
    for h in range(2):
        over[0][h].wait_recv()
        keep(0, h, plus(core_sum(3, h, 0), decode(got[4 + h])))
        keep(1, h, core_sum(3, h, 1))
    onward_send(1)
    for cp in out2:
        cp.wait_recv()
    full = diag_ref[...]
    state[:, :PANEL] = 0.5 * (full + full.T)
    state[:, PANEL:] = jnp.where(
        lax.broadcasted_iota(jnp.int32, (PANEL, PANEL), 0) == lax.broadcasted_iota(jnp.int32, (PANEL, PANEL), 1),
        1.0, 0.0,
    )
    z_out = []
    for h in range(2):
        onward[0][h].wait_recv()
        cp = ship(12 + h, plus(kept(0, h), decode(got[8 + h])), z1)
        cp.start()
        z_out.append(cp)
    invert_blocks(state, inv_ref, 0, 2)
    for h in range(2):
        over[1][h].wait_recv()
        keep(1, h, plus(kept(1, h), decode(got[6 + h])))
    for h in range(2):
        onward[1][h].wait_recv()
        keep(1, h, plus(kept(1, h), decode(got[10 + h])))
    invert_blocks(state, inv_ref, 2, 4)
    for h in range(2):
        z_out[h].wait_recv()
        cp = ship(14 + h, plus(kept(1, h), decode(got[12 + h])), z2)
        cp.start()
        z_out.append(cp)
    invert_blocks(state, inv_ref, 4, 8)

    f = panel_ref[0]
    block = (s * 4 + r) * 8
    for h in range(2):
        z_out[2 + h].wait_recv()
        mine, theirs = decode(coded[14 + h]), decode(got[14 + h])
        for t in range(2):
            tile = block + 4 * h + 2 * par + t
            piece = jnp.where(tile == f, full, mine[t] + theirs[t])
            part = lax.dot_general(
                piece, inv_ref[...], (((0,), (1,)), ((), ())),
                preferred_element_type=F32, precision=lax.Precision.HIGHEST,
            )

            @pl.when(hi == h)
            def _():
                factor_ref[t * PANEL : (t + 1) * PANEL, :] = jnp.where(tile >= f, part, 0.0)

            at = pl.ds(pl.multiple_of((4 * h + 2 * par + t) * PANEL, PANEL), PANEL)
            rows_ref[at, :] = jnp.where(tile > f, part, 0.0).astype(BF16)
    gather_phase(rows_ref, cols_ref, *gather_sems)
    for cp in core_copy + out1 + out2 + far[0] + far[1] + over[0] + over[1] + onward[0] + onward[1] + z_out:
        cp.wait_send()
    for cp in root_copy:
        cp.wait()


def panel_factor(panel_index, tiles, diag, root_matrix):
    row_block, col_block = root_matrix.shape
    tile = tiles.shape[1:]
    vmem = pl.BlockSpec(memory_space=pltpu.VMEM)
    dma = pltpu.SemaphoreType.DMA
    return pl.pallas_call(
        panel_kernel,
        out_shape=(
            pltpu.VMEM((2 * PANEL, PANEL), F32),
            pltpu.VMEM((row_block, PANEL), BF16),
            pltpu.VMEM((col_block, PANEL), BF16),
            pltpu.VMEM((row_block, col_block), F32),
        ),
        in_specs=[pl.BlockSpec(memory_space=pltpu.SMEM), vmem, vmem, pl.BlockSpec(memory_space=pltpu.HBM)],
        out_specs=(vmem, vmem, vmem, vmem),
        scratch_shapes=[
            pltpu.VMEM((4, 8, *tile), F32),
            pltpu.VMEM((2, 2, 2, *tile), F32),
            pltpu.VMEM((16, CODED, PANEL), jnp.int16),
            pltpu.VMEM((16, CODED, PANEL), jnp.int16),
            pltpu.VMEM(tile, F32),
            pltpu.VMEM(tile, F32),
            pltpu.VMEM((8, PANEL), F32),
            pltpu.VMEM((16, 8, PANEL), F32),
            pltpu.VMEM(tile, F32),
            pltpu.VMEM((PANEL, 2 * PANEL), F32),
            pltpu.VMEM(tile, F32),
            dma((4,)),
            dma((4,)),
            dma((16,)),
            dma((16,)),
            dma((4,)),
            dma((31,)),
            dma((31,)),
            dma((2,)),
            dma((2,)),
            *[dma((4,))] * 5,
        ],
        compiler_params=pltpu.CompilerParams(collective_id=0, has_side_effects=True, vmem_limit_bytes=40 * 2**20),
        name="panel_factor",
    )(panel_index, tiles, diag, root_matrix)


def trailing_kernel(root_ref, rows_ref, cols_ref, factor_ref, out_hbm, factor_hbm, held, sems):
    count = held.shape[0]
    rows = held.shape[1]
    copies = [pltpu.make_async_copy(factor_ref, factor_hbm, sems.at[count])]
    copies[0].start()
    for i in range(count):
        part = pl.ds(i * rows, rows)
        held[i] = root_ref[part, :] - lax.dot_general(
            rows_ref[part, :], cols_ref[...], (((1,), (1,)), ((), ())), preferred_element_type=F32
        )
        cp = pltpu.make_async_copy(held.at[i], out_hbm.at[part], sems.at[i])
        cp.start()
        copies.append(cp)
    for cp in copies:
        cp.wait()


def trailing_update(root, rows, cols, factor):
    hbm = pl.BlockSpec(memory_space=pltpu.HBM)
    vmem = pl.BlockSpec(memory_space=pltpu.VMEM)
    chunks = 8
    return pl.pallas_call(
        trailing_kernel,
        out_shape=(
            jax.ShapeDtypeStruct(root.shape, F32),
            jax.ShapeDtypeStruct(factor.shape, F32),
        ),
        in_specs=[vmem] * 4,
        out_specs=(hbm, hbm),
        scratch_shapes=[
            pltpu.VMEM((chunks, root.shape[0] // chunks, root.shape[1]), F32),
            pltpu.SemaphoreType.DMA((chunks + 1,)),
        ],
        compiler_params=pltpu.CompilerParams(vmem_limit_bytes=40 * 2**20),
        name="trailing_update",
    )(root, rows, cols, factor)


def direct(root_matrix, inverse_block, link_tiles, tile_mask, panel_index):
    tiles, diag = scenario_tiles(root_matrix, inverse_block[0], link_tiles[0], tile_mask, panel_index)
    factor, rows, cols, root = panel_factor(panel_index, tiles, diag, root_matrix)
    return trailing_update(root, rows, cols, factor)


def solution(mesh):
    in_specs = (
        P(("scen", "row"), "col"),
        P(("scen", "row", "col"), None, None),
        P(("scen", "row", "col"), None, None, None),
        P(("scen", "row", "col"), None),
        P(),
    )
    out_specs = (P(("scen", "row"), "col"), P(("scen", "row", "col"), None))
    sizes = tuple(mesh.shape[a] for a in ("scen", "row", "col"))
    body = direct if sizes == (2, 4, 4) else local
    return jax.shard_map(body, mesh=mesh, in_specs=in_specs, out_specs=out_specs, check_vma=False)
```

```python
import jax
import jax.numpy as jnp
from jax import lax
from jax.experimental import pallas as pl
from jax.experimental.pallas import tpu as pltpu
from jax.sharding import PartitionSpec as P

PANEL = 128


def broadcast(block, axis, source):
    block = jnp.where(lax.axis_index(axis) == source, block, jnp.zeros_like(block))
    return lax.psum(block, axis)


def select_matrix(tile_flags, slot_count):
    tile_ids = jnp.arange(tile_flags.shape[0])
    slot_order = jnp.sum(jnp.where(tile_ids[None, :] <= tile_ids[:, None], tile_flags[None, :], 0), axis=1) - 1
    slot_ids = lax.broadcasted_iota(jnp.int32, (slot_count, tile_flags.shape[0]), 0)
    hit = (slot_order[None, :] == slot_ids) & (tile_flags[None, :] == 1)
    return jnp.where(hit, jnp.float32(1.0), jnp.float32(0.0))


def compact_term(inverse, tiles_here, tile_flags, panel_at):
    slot_count, inner_rows, tile_rows = tiles_here.shape
    selector = select_matrix(tile_flags, slot_count)
    per_panel = PANEL // tile_rows
    picked = lax.dynamic_slice_in_dim(selector, panel_at * per_panel, per_panel, 1)
    columns = jnp.einsum(
        "kj,knt->njt", picked.astype(jnp.bfloat16), tiles_here, preferred_element_type=jnp.float32
    )
    columns = columns.reshape(inner_rows, PANEL).astype(jnp.bfloat16)
    weighted = jnp.dot(inverse, columns, preferred_element_type=jnp.float32).astype(jnp.bfloat16)
    product = jnp.einsum("knt,na->kta", tiles_here, weighted, preferred_element_type=jnp.float32)
    return (selector, product)


def dense_term(selector, product, base_cols, base_start):
    spread = jnp.einsum("kr,kta->rta", selector, product, precision=lax.Precision.HIGHEST)
    scenario = spread.reshape(selector.shape[1] * product.shape[1], PANEL)
    own_block = lax.dynamic_slice_in_dim(scenario, base_start, base_cols.shape[0], 0) + base_cols
    return lax.dynamic_update_slice_in_dim(scenario, own_block, base_start, 0)


def lower_rows(diagonal, rows_here, first_row, first_col):
    chol_lower = jnp.linalg.cholesky(diagonal)
    solved = jax.scipy.linalg.solve_triangular(chol_lower, rows_here.T, lower=True).T
    row_ids = first_row + lax.broadcasted_iota(jnp.int32, (rows_here.shape[0], 1), 0)
    return jnp.where(row_ids >= first_col, solved, 0.0)


def trailing_rows(factor_part, first_row, first_col):
    rounded = factor_part.astype(jnp.bfloat16)
    row_ids = first_row + lax.broadcasted_iota(jnp.int32, (factor_part.shape[0], 1), 0)
    return jnp.where(row_ids >= first_col + PANEL, rounded, jnp.zeros_like(rounded))


def local(root_matrix, inverse_block, link_tiles, tile_mask, panel_index):
    panel_at = panel_index[0]
    tile_flags = tile_mask[0]
    selector, product = compact_term(inverse_block[0], link_tiles[0], tile_flags, panel_at)
    tile_count = selector.shape[1]
    tile_rows = product.shape[1]
    total_rows = tile_count * tile_rows
    row_block, col_block = root_matrix.shape
    scen_at = lax.axis_index("scen")
    row_at = lax.axis_index("row")
    col_at = lax.axis_index("col")
    row_count = lax.axis_size("row")
    col_count = lax.axis_size("col")
    scen_count = lax.axis_size("scen")
    block_at = scen_at * row_count + row_at
    first_col = panel_at * PANEL
    owner_col = first_col // col_block
    base_cols = lax.dynamic_slice_in_dim(root_matrix, first_col - owner_col * col_block, PANEL, 1)
    base_cols = jnp.where(col_at == owner_col, base_cols, 0.0)
    piece_rows = row_block // col_count
    scenario = dense_term(selector, product, base_cols, block_at * row_block)
    slab_rows = total_rows // scen_count
    slab_sum = lax.psum_scatter(scenario, "scen", scatter_dimension=0, tiled=True)
    slab_sum = lax.psum(slab_sum, ("row", "col"))
    owner_slab = first_col // slab_rows
    diag_part = lax.dynamic_slice_in_dim(slab_sum, first_col - owner_slab * slab_rows, PANEL, 0)
    diagonal = broadcast(diag_part, "scen", owner_slab)
    slab_first = scen_at * slab_rows
    slab_factor = lower_rows(diagonal, slab_sum, slab_first, first_col)
    factor_rows = lax.dynamic_slice_in_dim(
        slab_factor, (row_at * col_count + col_at) * piece_rows, piece_rows, 0
    )
    ending = trailing_rows(slab_factor, slab_first, first_col)
    all_factor = lax.all_gather(ending, "scen", axis=0, tiled=True)
    own_rows = lax.dynamic_slice_in_dim(all_factor, block_at * row_block, row_block, 0)
    own_cols = lax.dynamic_slice_in_dim(all_factor, col_at * col_block, col_block, 0)
    update = lax.dot_general(
        own_rows, own_cols, (((1,), (1,)), ((), ())), preferred_element_type=jnp.float32
    )
    return (root_matrix - update, factor_rows)


MESH_ID = pl.DeviceIdType.MESH
F32 = jnp.float32
BF16 = jnp.bfloat16


def remote(src, dst, send, recv, device):
    return pltpu.make_async_remote_copy(
        src_ref=src, dst_ref=dst, send_sem=send, recv_sem=recv, device_id=device, device_id_type=MESH_ID
    )


BLOCK = 16
CODED = 2 * PANEL + 16


def invert_blocks(state, inv_ref, start, stop):
    lane = lax.broadcasted_iota(jnp.int32, (BLOCK, PANEL), 1)
    sub = lax.broadcasted_iota(jnp.int32, (BLOCK, PANEL), 0)

    def block(b, carry):
        at = pl.ds(pl.multiple_of(b * BLOCK, BLOCK), BLOCK)
        left, right = state[at, :PANEL], state[at, PANEL:]
        cols = [
            jnp.broadcast_to(
                jnp.sum(jnp.where(lane == b * BLOCK + j, left, 0.0), axis=1, keepdims=True), (BLOCK, PANEL)
            )
            for j in range(BLOCK)
        ]
        for i in range(BLOCK):
            pivot = cols[i][i : i + 1, :]
            inv = lax.rsqrt(pivot)
            inv = inv * (1.5 - 0.5 * pivot * inv * inv)
            coef = jnp.where(sub > i, cols[i] * inv, 0.0)
            for j in range(i + 1, BLOCK):
                cols[j] = cols[j] - coef * (cols[j][i : i + 1, :] * inv)
            row_l, row_r = left[i : i + 1, :] * inv, right[i : i + 1, :] * inv
            left = jnp.where(sub == i, row_l, left - coef * row_l)
            right = jnp.where(sub == i, row_r, right - coef * row_r)
        inv_ref[at, :] = right
        later = jnp.where(lane >= b * BLOCK + BLOCK, left, 0.0)
        state[...] = state[...] - lax.dot_general(
            later, jnp.concatenate([left, right], axis=1), (((0,), (0,)), ((), ())),
            preferred_element_type=F32, precision=lax.Precision.HIGHEST,
        )
        return carry

    lax.fori_loop(start, stop, block, 0)


def code_scale(exponent):
    return jnp.exp2(15.0 - exponent) * 0.995


def encode(pair, out):
    exps = []
    for t in range(2):
        top = jnp.max(jnp.abs(pair[t]), axis=0, keepdims=True)
        exponent = jnp.ceil(jnp.log2(jnp.maximum(top, 1e-30)))
        out[t * PANEL : (t + 1) * PANEL, :] = jnp.round(pair[t] * code_scale(exponent)).astype(jnp.int32).astype(jnp.int16)
        exps.append(jnp.broadcast_to(exponent, (8, PANEL)))
    out[2 * PANEL : CODED, :] = jnp.concatenate(exps, axis=0).astype(jnp.int32).astype(jnp.int16)


def decode(coded):
    exponent = coded[2 * PANEL : CODED, :].astype(jnp.int32).astype(F32)
    return [
        coded[t * PANEL : (t + 1) * PANEL, :].astype(jnp.int32).astype(F32)
        * (1.0 / code_scale(exponent[8 * t : 8 * t + 1, :]))
        for t in range(2)
    ]


def gather_phase(solve, rows_ref, cols_ref, send_z, recv_z, send_x, send_y, recv_p, send_c, recv_c):
    s, r, c = (lax.axis_index(a) for a in ("scen", "row", "col"))
    y, k = r // 2, lax.rem(r, 2)
    rows = 2 * PANEL
    far_x = lax.rem(s + c // 2, 2)
    far_y = lax.rem(y + c, 2)
    source = jnp.logical_and(far_x == 0, far_y == 0)
    x_to = (1 - s, r, c)
    y_to = (s, 2 * (1 - y) + k, c)
    z1 = (s, r, c + 1 - 2 * lax.rem(c, 2))
    core = (s, 2 * y + 1 - k, c)
    par = lax.rem(c, 2)
    pieces = (par, par + 2, 1 - par, 3 - par)

    def row_at(z):
        return rows_ref.at[pl.ds(pl.multiple_of(z * rows, rows), rows)]

    def col_at(kk, z):
        return cols_ref.at[pl.ds(pl.multiple_of((kk * 4 + z) * rows, rows), rows)]

    def z_copy(i):
        return remote(row_at(pieces[i]), row_at(pieces[i]), send_z.at[i], recv_z.at[i], z1)

    def z_arrival(i):
        return remote(row_at(pieces[2 + i]), row_at(pieces[2 + i]), send_z.at[i], recv_z.at[i], z1)

    def first_hop(o, to, sems):
        return remote(row_at(pieces[o]), col_at(k, pieces[o]), sems.at[o], recv_p.at[o], to)

    def onward(o):
        here = col_at(k, pieces[o])
        return remote(here, here, (send_x if o % 2 else send_y).at[o], recv_p.at[o], x_to if o % 2 else y_to)

    def forwards(o):
        if o % 2:
            return jnp.logical_and(far_x == 0, far_y == 1)
        return jnp.logical_and(far_x == 1, far_y == 0)

    def to_core(o, kk):
        here = col_at(kk, pieces[o])
        return remote(here, here, send_c.at[o], recv_c.at[o], core)

    def begin(o):
        @pl.when(source)
        def _():
            first_hop(o, x_to, send_x).start()
            first_hop(o, y_to, send_y).start()

        z_copy(o).start()

    for o in range(2):
        solve(o)
        begin(o)

    for o in range(4):

        @pl.when(source)
        def _():
            if o >= 2:
                z_arrival(o - 2).wait_recv()
                first_hop(o, x_to, send_x).start()
                first_hop(o, y_to, send_y).start()
            col_at(k, pieces[o])[...] = row_at(pieces[o])[...]

        @pl.when(jnp.logical_not(source))
        def _():
            onward(o).wait_recv()

        @pl.when(forwards(o))
        def _():
            onward(o).start()

        to_core(o, k).start()

    @pl.when(jnp.logical_not(source))
    def _():
        for i in range(2):
            z_arrival(i).wait_recv()

    for o in range(4):
        to_core(o, 1 - k).wait_recv()
        to_core(o, k).wait_send()

        @pl.when(source)
        def _():
            first_hop(o, x_to, send_x).wait_send()
            first_hop(o, y_to, send_y).wait_send()

        @pl.when(forwards(o))
        def _():
            onward(o).wait_send()

    for i in range(2):
        z_copy(i).wait_send()


def panel_kernel(panel_ref, mask_ref, inv_hbm, tiles_hbm, root_hbm, factor_ref, rows_ref, cols_ref, root_ref,
                 given, tiles, prod, lent, slot_ref, got0, acc, coded, got, base, dmine, dsum, dgot, dpart, dparts, diag_ref,
                 state, inv_ref, load_sem, core_send, core_recv, send, recv, root_sem, dsend, drecv, *gather_sems):
    s, r, c = (lax.axis_index(a) for a in ("scen", "row", "col"))
    y, k = r // 2, lax.rem(r, 2)
    core = (s, 2 * y + 1 - k, c)
    x_to = (1 - s, r, c)
    y_to = (s, 2 * (1 - y) + k, c)
    par = lax.rem(c, 2)
    hi = c // 2
    z1 = (s, r, c + 1 - 2 * par)
    z2 = (s, r, lax.rem(c + 2, 4))
    me = s * 8 + y * 4 + c
    f = panel_ref[0]
    block = (s * 4 + r) * 8
    slots = tiles.shape[0]
    some = slots // 4
    wide = root_ref.shape[1] // PANEL

    loads = []
    for i in range(4):
        at = pl.ds(i * some, some)
        loads.append(pltpu.make_async_copy(tiles_hbm.at[at], tiles.at[at], load_sem.at[i]))
    loads.append(pltpu.make_async_copy(inv_hbm, given, load_sem.at[4]))
    for cp in loads:
        cp.start()

    def chip(o):
        q = lax.rem(me + o, 16)
        return q, (q // 8, 2 * lax.rem(q // 4, 2) + k, lax.rem(q, 4))

    barrier = pltpu.get_barrier_semaphore()
    pl.semaphore_signal(barrier, inc=1, device_id=core, device_id_type=MESH_ID)
    for o in range(1, 16):
        pl.semaphore_signal(barrier, inc=1, device_id=chip(o)[1], device_id_type=MESH_ID)

    def place(t, at):
        flag = mask_ref[0, t]
        slot_ref[t] = jnp.where(flag == 1, at, slots)
        return at + flag

    lax.fori_loop(0, mask_ref.shape[1], place, 0)
    prod[slots] = jnp.zeros(prod.shape[1:], F32)
    for cp in loads[:4]:
        cp.wait()
    panel_slot = slot_ref[f]
    columns = tiles[jnp.minimum(panel_slot, slots - 1)]
    columns = jnp.where(panel_slot < slots, columns, jnp.zeros_like(columns))
    loads[4].wait()
    root_copy = []
    for i in range(4):
        part = pl.ds(i * (root_ref.shape[0] // 4), root_ref.shape[0] // 4)
        cp = pltpu.make_async_copy(root_hbm.at[part], root_ref.at[part], root_sem.at[i])
        cp.start()
        root_copy.append(cp)
    weighted = lax.dot_general(
        columns, given[...], (((0,), (0,)), ((), ())), preferred_element_type=F32
    ).astype(BF16)
    for i in range(slots // 2):
        both = jnp.dot(
            weighted, jnp.concatenate([tiles[2 * i], tiles[2 * i + 1]], axis=1), preferred_element_type=F32
        )
        prod[2 * i] = both[:, :PANEL]
        prod[2 * i + 1] = both[:, PANEL:]

    pl.semaphore_wait(barrier, 16)
    order = ((1 - s) * 2 + 1 - y, (1 - s) * 2 + y, s * 2 + 1 - y, s * 2 + y)
    core_copy = []
    for n, i in enumerate(order):
        for t in range(8):
            lent[n, t] = prod[slot_ref[(i * 2 + 1 - k) * 8 + t]]
        cp = remote(lent.at[n], got0.at[n], core_send.at[n], core_recv.at[n], core)
        cp.start()
        core_copy.append(cp)

    pair = (2 * (1 - par), 2 * par)

    def core_sum(n, h, j):
        at = [4 * h + pair[j] + t for t in range(2)]
        return [prod[slot_ref[(order[n] * 2 + k) * 8 + a]] + got0[n, a] for a in at]

    def plus(a, b):
        return [a[t] + b[t] for t in range(2)]

    def ship(at, value, to):
        encode(value, coded.at[at])
        return remote(coded.at[at], got.at[at], send.at[at], recv.at[at], to)

    ways = (x_to, y_to)
    far, over, onward = ([[None, None], [None, None]] for _ in range(3))

    def far_send(j):
        for h in range(2):
            far[j][h] = ship(j * 2 + h, core_sum(0, h, j), ways[h])
            far[j][h].start()

    def over_make(j):
        for h in range(2):
            over[j][h] = ship(4 + j * 2 + h, core_sum(1 + h, h, j), ways[h])

    def onward_send(j):
        for h in range(2):
            far[j][h].wait_recv()
            value = plus(core_sum(2 - h, h, j), decode(got[j * 2 + h]))
            onward[j][h] = ship(8 + j * 2 + h, value, ways[1 - h])
            onward[j][h].start()

    def based(h, j):
        return plus(core_sum(3, h, j), [base[4 * h + pair[j] + t] for t in range(2)])

    def keep(j, h, value):
        for t in range(2):
            acc[j, h, t] = value[t]

    def kept(j, h):
        return [acc[j, h, t] for t in range(2)]

    core_copy[0].wait_recv()
    far_send(0)
    core_copy[1].wait_recv()
    core_copy[2].wait_recv()
    over_make(0)
    for h in range(2):
        over[0][h].start()
    far_send(1)
    over_make(1)

    for cp in root_copy:
        cp.wait()
    lane_block = lax.rem(f, wide)
    owner = c == f // wide

    def fetch_base(t, carry):
        at = pl.ds(pl.multiple_of(t * PANEL, PANEL), PANEL)
        value = jnp.zeros((PANEL, PANEL), F32)
        for j in range(wide):
            here = jnp.logical_and(owner, lane_block == j)
            value = jnp.where(here, root_ref[at, j * PANEL : (j + 1) * PANEL], value)
        base[t] = value.T
        return carry

    lax.fori_loop(0, 8, fetch_base, 0)
    own_diag = prod[slot_ref[f]]
    for t in range(8):
        own_diag = own_diag + jnp.where(block + t == f, base[t], 0.0)
    dmine[...] = own_diag
    core_diag = remote(dmine, dgot, dsend.at[0], drecv.at[0], core)
    core_diag.start()
    core_diag.wait()
    dsum[...] = dmine[...] + dgot[...]
    out1 = []
    for o in range(1, 16):
        q, dev = chip(o)
        cp = remote(dsum.at[pl.ds(pl.multiple_of(q * 8, 8), 8)], dparts.at[o], dsend.at[o], drecv.at[o], dev)
        cp.start()
        out1.append(cp)

    onward_send(0)
    for h in range(2):
        over[1][h].start()
    core_copy[3].wait_recv()
    for h in range(2):
        over[0][h].wait_recv()
        keep(0, h, plus(based(h, 0), decode(got[4 + h])))
        keep(1, h, based(h, 1))
    for cp in out1:
        cp.wait_recv()
    total = dsum[pl.ds(pl.multiple_of(me * 8, 8), 8), :]
    for o in range(1, 16):
        total = total + dparts[o]
    dpart[...] = total
    diag_ref[pl.ds(pl.multiple_of(me * 8, 8), 8), :] = total
    out2 = []
    for o in range(1, 16):
        q, dev = chip(o)
        cp = remote(dpart, diag_ref.at[pl.ds(pl.multiple_of(me * 8, 8), 8)], dsend.at[15 + o], drecv.at[15 + o], dev)
        cp.start()
        out2.append(cp)
    onward_send(1)
    z_out = []
    for h in range(2):
        onward[0][h].wait_recv()
        cp = ship(12 + h, plus(kept(0, h), decode(got[8 + h])), z1)
        cp.start()
        z_out.append(cp)
    for h in range(2):
        over[1][h].wait_recv()
        keep(1, h, plus(kept(1, h), decode(got[6 + h])))
    for h in range(2):
        onward[1][h].wait_recv()
        keep(1, h, plus(kept(1, h), decode(got[10 + h])))

    for h in range(2):
        z_out[h].wait_recv()
        cp = ship(14 + h, plus(kept(1, h), decode(got[12 + h])), z2)
        cp.start()
        z_out.append(cp)
    for cp in out2:
        cp.wait_recv()
    full = diag_ref[...]
    state[:, :PANEL] = 0.5 * (full + full.T)
    state[:, PANEL:] = jnp.where(
        lax.broadcasted_iota(jnp.int32, (PANEL, PANEL), 0) == lax.broadcasted_iota(jnp.int32, (PANEL, PANEL), 1),
        1.0, 0.0,
    )
    invert_blocks(state, inv_ref, 0, 8)

    def solve(h):
        z_out[2 + h].wait_recv()
        mine, theirs = decode(coded[14 + h]), decode(got[14 + h])
        for t in range(2):
            tile = block + 4 * h + 2 * par + t
            piece = jnp.where(tile == f, full, mine[t] + theirs[t])
            part = lax.dot_general(
                piece, inv_ref[...], (((0,), (1,)), ((), ())),
                preferred_element_type=F32, precision=lax.Precision.HIGHEST,
            )

            @pl.when(hi == h)
            def _():
                factor_ref[t * PANEL : (t + 1) * PANEL, :] = jnp.where(tile >= f, part, 0.0)

            at = pl.ds(pl.multiple_of((4 * h + 2 * par + t) * PANEL, PANEL), PANEL)
            rows_ref[at, :] = jnp.where(tile > f, part, 0.0).astype(BF16)

    gather_phase(solve, rows_ref, cols_ref, *gather_sems)
    for cp in core_copy + out1 + out2 + far[0] + far[1] + over[0] + over[1] + onward[0] + onward[1] + z_out:
        cp.wait_send()


def panel_factor(panel_index, tile_mask, inverse, tiles, root_matrix):
    row_block, col_block = root_matrix.shape
    slots, inner, tile_rows = tiles.shape
    tile = (PANEL, tile_rows)
    smem = pl.BlockSpec(memory_space=pltpu.SMEM)
    hbm = pl.BlockSpec(memory_space=pltpu.HBM)
    vmem = pl.BlockSpec(memory_space=pltpu.VMEM)
    dma = pltpu.SemaphoreType.DMA
    return pl.pallas_call(
        panel_kernel,
        out_shape=(
            pltpu.VMEM((2 * PANEL, PANEL), F32),
            pltpu.VMEM((row_block, PANEL), BF16),
            pltpu.VMEM((col_block, PANEL), BF16),
            pltpu.VMEM((row_block, col_block), F32),
        ),
        in_specs=[smem, smem, hbm, hbm, hbm],
        out_specs=(vmem, vmem, vmem, vmem),
        scratch_shapes=[
            pltpu.VMEM(inverse.shape, BF16),
            pltpu.VMEM(tiles.shape, BF16),
            pltpu.VMEM((slots + 1, *tile), F32),
            pltpu.VMEM((4, 8, *tile), F32),
            pltpu.SMEM((tile_mask.shape[1],), jnp.int32),
            pltpu.VMEM((4, 8, *tile), F32),
            pltpu.VMEM((2, 2, 2, *tile), F32),
            pltpu.VMEM((16, CODED, PANEL), jnp.int16),
            pltpu.VMEM((16, CODED, PANEL), jnp.int16),
            pltpu.VMEM((8, *tile), F32),
            pltpu.VMEM(tile, F32),
            pltpu.VMEM(tile, F32),
            pltpu.VMEM(tile, F32),
            pltpu.VMEM((8, PANEL), F32),
            pltpu.VMEM((16, 8, PANEL), F32),
            pltpu.VMEM(tile, F32),
            pltpu.VMEM((PANEL, 2 * PANEL), F32),
            pltpu.VMEM(tile, F32),
            dma((5,)),
            dma((4,)),
            dma((4,)),
            dma((16,)),
            dma((16,)),
            dma((4,)),
            dma((31,)),
            dma((31,)),
            dma((2,)),
            dma((2,)),
            *[dma((4,))] * 5,
        ],
        compiler_params=pltpu.CompilerParams(collective_id=0, has_side_effects=True, vmem_limit_bytes=54 * 2**20),
        name="panel_factor",
    )(panel_index, tile_mask, inverse, tiles, root_matrix)


def trailing_kernel(root_ref, rows_ref, cols_ref, factor_ref, out_hbm, factor_hbm, held, sems):
    count = held.shape[0]
    rows = held.shape[1]
    copies = [pltpu.make_async_copy(factor_ref, factor_hbm, sems.at[count])]
    copies[0].start()
    for i in range(count):
        part = pl.ds(i * rows, rows)
        held[i] = root_ref[part, :] - lax.dot_general(
            rows_ref[part, :], cols_ref[...], (((1,), (1,)), ((), ())), preferred_element_type=F32
        )
        cp = pltpu.make_async_copy(held.at[i], out_hbm.at[part], sems.at[i])
        cp.start()
        copies.append(cp)
    for cp in copies:
        cp.wait()


def trailing_update(root, rows, cols, factor):
    hbm = pl.BlockSpec(memory_space=pltpu.HBM)
    vmem = pl.BlockSpec(memory_space=pltpu.VMEM)
    chunks = 8
    return pl.pallas_call(
        trailing_kernel,
        out_shape=(
            jax.ShapeDtypeStruct(root.shape, F32),
            jax.ShapeDtypeStruct(factor.shape, F32),
        ),
        in_specs=[vmem] * 4,
        out_specs=(hbm, hbm),
        scratch_shapes=[
            pltpu.VMEM((chunks, root.shape[0] // chunks, root.shape[1]), F32),
            pltpu.SemaphoreType.DMA((chunks + 1,)),
        ],
        compiler_params=pltpu.CompilerParams(vmem_limit_bytes=40 * 2**20),
        name="trailing_update",
    )(root, rows, cols, factor)


def direct(root_matrix, inverse_block, link_tiles, tile_mask, panel_index):
    factor, rows, cols, root = panel_factor(panel_index, tile_mask, inverse_block[0], link_tiles[0], root_matrix)
    return trailing_update(root, rows, cols, factor)


def solution(mesh):
    in_specs = (
        P(("scen", "row"), "col"),
        P(("scen", "row", "col"), None, None),
        P(("scen", "row", "col"), None, None, None),
        P(("scen", "row", "col"), None),
        P(),
    )
    out_specs = (P(("scen", "row"), "col"), P(("scen", "row", "col"), None))
    sizes = tuple(mesh.shape[a] for a in ("scen", "row", "col"))
    body = direct if sizes == (2, 4, 4) else local
    return jax.shard_map(body, mesh=mesh, in_specs=in_specs, out_specs=out_specs, check_vma=False)
```

```python
import jax
import jax.numpy as jnp
from jax import lax
from jax.experimental import pallas as pl
from jax.experimental.pallas import tpu as pltpu
from jax.sharding import PartitionSpec as P

PANEL = 128


def broadcast(block, axis, source):
    block = jnp.where(lax.axis_index(axis) == source, block, jnp.zeros_like(block))
    return lax.psum(block, axis)


def select_matrix(tile_flags, slot_count):
    tile_ids = jnp.arange(tile_flags.shape[0])
    slot_order = jnp.sum(jnp.where(tile_ids[None, :] <= tile_ids[:, None], tile_flags[None, :], 0), axis=1) - 1
    slot_ids = lax.broadcasted_iota(jnp.int32, (slot_count, tile_flags.shape[0]), 0)
    hit = (slot_order[None, :] == slot_ids) & (tile_flags[None, :] == 1)
    return jnp.where(hit, jnp.float32(1.0), jnp.float32(0.0))


def compact_term(inverse, tiles_here, tile_flags, panel_at):
    slot_count, inner_rows, tile_rows = tiles_here.shape
    selector = select_matrix(tile_flags, slot_count)
    per_panel = PANEL // tile_rows
    picked = lax.dynamic_slice_in_dim(selector, panel_at * per_panel, per_panel, 1)
    columns = jnp.einsum(
        "kj,knt->njt", picked.astype(jnp.bfloat16), tiles_here, preferred_element_type=jnp.float32
    )
    columns = columns.reshape(inner_rows, PANEL).astype(jnp.bfloat16)
    weighted = jnp.dot(inverse, columns, preferred_element_type=jnp.float32).astype(jnp.bfloat16)
    product = jnp.einsum("knt,na->kta", tiles_here, weighted, preferred_element_type=jnp.float32)
    return (selector, product)


def dense_term(selector, product, base_cols, base_start):
    spread = jnp.einsum("kr,kta->rta", selector, product, precision=lax.Precision.HIGHEST)
    scenario = spread.reshape(selector.shape[1] * product.shape[1], PANEL)
    own_block = lax.dynamic_slice_in_dim(scenario, base_start, base_cols.shape[0], 0) + base_cols
    return lax.dynamic_update_slice_in_dim(scenario, own_block, base_start, 0)


def lower_rows(diagonal, rows_here, first_row, first_col):
    chol_lower = jnp.linalg.cholesky(diagonal)
    solved = jax.scipy.linalg.solve_triangular(chol_lower, rows_here.T, lower=True).T
    row_ids = first_row + lax.broadcasted_iota(jnp.int32, (rows_here.shape[0], 1), 0)
    return jnp.where(row_ids >= first_col, solved, 0.0)


def trailing_rows(factor_part, first_row, first_col):
    rounded = factor_part.astype(jnp.bfloat16)
    row_ids = first_row + lax.broadcasted_iota(jnp.int32, (factor_part.shape[0], 1), 0)
    return jnp.where(row_ids >= first_col + PANEL, rounded, jnp.zeros_like(rounded))


def local(root_matrix, inverse_block, link_tiles, tile_mask, panel_index):
    panel_at = panel_index[0]
    tile_flags = tile_mask[0]
    selector, product = compact_term(inverse_block[0], link_tiles[0], tile_flags, panel_at)
    tile_count = selector.shape[1]
    tile_rows = product.shape[1]
    total_rows = tile_count * tile_rows
    row_block, col_block = root_matrix.shape
    scen_at = lax.axis_index("scen")
    row_at = lax.axis_index("row")
    col_at = lax.axis_index("col")
    row_count = lax.axis_size("row")
    col_count = lax.axis_size("col")
    scen_count = lax.axis_size("scen")
    block_at = scen_at * row_count + row_at
    first_col = panel_at * PANEL
    owner_col = first_col // col_block
    base_cols = lax.dynamic_slice_in_dim(root_matrix, first_col - owner_col * col_block, PANEL, 1)
    base_cols = jnp.where(col_at == owner_col, base_cols, 0.0)
    piece_rows = row_block // col_count
    scenario = dense_term(selector, product, base_cols, block_at * row_block)
    slab_rows = total_rows // scen_count
    slab_sum = lax.psum_scatter(scenario, "scen", scatter_dimension=0, tiled=True)
    slab_sum = lax.psum(slab_sum, ("row", "col"))
    owner_slab = first_col // slab_rows
    diag_part = lax.dynamic_slice_in_dim(slab_sum, first_col - owner_slab * slab_rows, PANEL, 0)
    diagonal = broadcast(diag_part, "scen", owner_slab)
    slab_first = scen_at * slab_rows
    slab_factor = lower_rows(diagonal, slab_sum, slab_first, first_col)
    factor_rows = lax.dynamic_slice_in_dim(
        slab_factor, (row_at * col_count + col_at) * piece_rows, piece_rows, 0
    )
    ending = trailing_rows(slab_factor, slab_first, first_col)
    all_factor = lax.all_gather(ending, "scen", axis=0, tiled=True)
    own_rows = lax.dynamic_slice_in_dim(all_factor, block_at * row_block, row_block, 0)
    own_cols = lax.dynamic_slice_in_dim(all_factor, col_at * col_block, col_block, 0)
    update = lax.dot_general(
        own_rows, own_cols, (((1,), (1,)), ((), ())), preferred_element_type=jnp.float32
    )
    return (root_matrix - update, factor_rows)


MESH_ID = pl.DeviceIdType.MESH
F32 = jnp.float32
BF16 = jnp.bfloat16


def remote(src, dst, send, recv, device):
    return pltpu.make_async_remote_copy(
        src_ref=src, dst_ref=dst, send_sem=send, recv_sem=recv, device_id=device, device_id_type=MESH_ID
    )


BLOCK = 16
CODED = 2 * PANEL + 16


def thirds(value):
    high = value.astype(BF16)
    rest = value - high.astype(F32)
    mid = rest.astype(BF16)
    return high, mid, (rest - mid.astype(F32)).astype(BF16)


TERMS = ((0, 0), (0, 1), (1, 0), (1, 1), (0, 2), (2, 0))


def stack(parts, side, axis):
    return jnp.concatenate([parts[term[side]] for term in TERMS], axis=axis)


def invert_blocks(state, inv_ref, start, stop):
    lane = lax.broadcasted_iota(jnp.int32, (BLOCK, PANEL), 1)
    sub = lax.broadcasted_iota(jnp.int32, (BLOCK, PANEL), 0)

    def block(b, carry):
        at = pl.ds(pl.multiple_of(b * BLOCK, BLOCK), BLOCK)
        left, right = state[at, :PANEL], state[at, PANEL:]
        cols = [
            jnp.broadcast_to(
                jnp.sum(jnp.where(lane == b * BLOCK + j, left, 0.0), axis=1, keepdims=True), (BLOCK, PANEL)
            )
            for j in range(BLOCK)
        ]
        for i in range(0, BLOCK, 2):
            first, cross, second = cols[i][i : i + 1, :], cols[i][i + 1 : i + 2, :], cols[i + 1][i + 1 : i + 2, :]
            det = first * second - cross * cross
            root_1, root_d = lax.rsqrt(first), lax.rsqrt(det)
            inv_1, inv_d = root_1 * root_1, root_d * root_d
            miss_1, miss_d = 1.0 - first * inv_1, 1.0 - det * inv_d
            root_1, inv_1 = root_1 + 0.5 * root_1 * miss_1, inv_1 + inv_1 * miss_1
            root_d, inv_d = root_d + 0.5 * root_d * miss_d, inv_d + inv_d * miss_d
            below_1 = jnp.where(sub > i + 1, cols[i], 0.0)
            below_2 = jnp.where(sub > i + 1, cols[i + 1], 0.0)
            coef_1 = (below_1 * second - below_2 * cross) * inv_d
            coef_2 = (below_2 * first - below_1 * cross) * inv_d
            for j in range(i + 2, BLOCK):
                cols[j] = cols[j] - (coef_1 * cols[j][i : i + 1, :] + coef_2 * cols[j][i + 1 : i + 2, :])
            root_2 = first * root_1 * root_d
            ratio = cross * inv_1

            def step(strip):
                row_1, row_2 = strip[i : i + 1, :], strip[i + 1 : i + 2, :]
                rest = strip - (coef_1 * row_1 + coef_2 * row_2)
                return jnp.where(
                    sub == i, row_1 * root_1, jnp.where(sub == i + 1, (row_2 - ratio * row_1) * root_2, rest)
                )

            left, right = step(left), step(right)
        inv_ref[at, :] = right
        later = thirds(jnp.where(lane >= b * BLOCK + BLOCK, left, 0.0))
        strip = thirds(jnp.concatenate([left, right], axis=1))
        state[...] = state[...] - lax.dot_general(
            stack(later, 0, 0), stack(strip, 1, 0), (((0,), (0,)), ((), ())), preferred_element_type=F32
        )
        return carry

    lax.fori_loop(start, stop, block, 0)


def code_scale(exponent):
    return jnp.exp2(15.0 - exponent) * 0.995


def encode(pair, out):
    exps = []
    for t in range(2):
        top = jnp.max(jnp.abs(pair[t]), axis=0, keepdims=True)
        exponent = jnp.ceil(jnp.log2(jnp.maximum(top, 1e-30)))
        out[t * PANEL : (t + 1) * PANEL, :] = jnp.round(pair[t] * code_scale(exponent)).astype(jnp.int32).astype(jnp.int16)
        exps.append(jnp.broadcast_to(exponent, (8, PANEL)))
    out[2 * PANEL : CODED, :] = jnp.concatenate(exps, axis=0).astype(jnp.int32).astype(jnp.int16)


def decode(coded):
    exponent = coded[2 * PANEL : CODED, :].astype(jnp.int32).astype(F32)
    return [
        coded[t * PANEL : (t + 1) * PANEL, :].astype(jnp.int32).astype(F32)
        * (1.0 / code_scale(exponent[8 * t : 8 * t + 1, :]))
        for t in range(2)
    ]


def gather_phase(solve, rows_ref, cols_ref, send_z, recv_z, send_x, send_y, recv_p, send_c, recv_c):
    s, r, c = (lax.axis_index(a) for a in ("scen", "row", "col"))
    y, k = r // 2, lax.rem(r, 2)
    rows = 2 * PANEL
    far_x = lax.rem(s + c // 2, 2)
    far_y = lax.rem(y + c, 2)
    source = jnp.logical_and(far_x == 0, far_y == 0)
    beside_y = jnp.logical_and(far_x == 0, far_y == 1)
    x_to = (1 - s, r, c)
    y_to = (s, 2 * (1 - y) + k, c)
    z1 = (s, r, c + 1 - 2 * lax.rem(c, 2))
    core = (s, 2 * y + 1 - k, c)
    par = lax.rem(c, 2)
    pieces = (par, par + 2, 1 - par, 3 - par)

    def row_at(z):
        return rows_ref.at[pl.ds(pl.multiple_of(z * rows, rows), rows)]

    def col_at(kk, z):
        return cols_ref.at[pl.ds(pl.multiple_of((kk * 4 + z) * rows, rows), rows)]

    def z_copy(i):
        return remote(row_at(pieces[i]), row_at(pieces[i]), send_z.at[i], recv_z.at[i], z1)

    def z_arrival(i):
        return remote(row_at(pieces[2 + i]), row_at(pieces[2 + i]), send_z.at[i], recv_z.at[i], z1)

    def first_hop(o, to, sems):
        return remote(row_at(pieces[o]), col_at(k, pieces[o]), sems.at[o], recv_p.at[o], to)

    def onward(o):
        here = col_at(k, pieces[o])
        return remote(here, here, (send_x if o % 2 else send_y).at[o], recv_p.at[o], x_to if o % 2 else y_to)

    def forwards(o):
        if o % 2:
            return jnp.logical_and(far_x == 0, far_y == 1)
        return jnp.logical_and(far_x == 1, far_y == 0)

    def to_core_first(o):
        remote(row_at(pieces[o]), col_at(k, pieces[o]), send_c.at[o], recv_c.at[o], core).start()

    def to_core(o, kk):
        here = col_at(kk, pieces[o])
        return remote(here, here, send_c.at[o], recv_c.at[o], core)

    def spread(a):
        first_hop(a, x_to, send_x).start()
        first_hop(a + 1, y_to, send_y).start()
        first_hop(a + 1, x_to, send_x).start()
        first_hop(a, y_to, send_y).start()

    def finish(o):
        onward(o).wait_recv()

        @pl.when(forwards(o))
        def _():
            onward(o).start()

        to_core(o, k).start()

    for o in range(2):
        solve(o)

        @pl.when(source)
        def _():
            if o == 1:
                spread(0)
            to_core_first(o)

        z_copy(o).start()

    for a in range(0, 4, 2):

        @pl.when(source)
        def _():
            if a:
                for i in range(2):
                    z_arrival(i).wait_recv()
                spread(a)
                for i in range(2):
                    to_core_first(a + i)
            for i in range(2):
                col_at(k, pieces[a + i])[...] = row_at(pieces[a + i])[...]

        @pl.when(jnp.logical_and(jnp.logical_not(source), jnp.logical_not(beside_y)))
        def _():
            finish(a)
            finish(a + 1)

        @pl.when(beside_y)
        def _():
            finish(a + 1)
            finish(a)

    @pl.when(jnp.logical_not(source))
    def _():
        for i in range(2):
            z_arrival(i).wait_recv()

    for o in range(4):
        to_core(o, 1 - k).wait_recv()
        to_core(o, k).wait_send()

        @pl.when(source)
        def _():
            first_hop(o, x_to, send_x).wait_send()
            first_hop(o, y_to, send_y).wait_send()

        @pl.when(forwards(o))
        def _():
            onward(o).wait_send()

    for i in range(2):
        z_copy(i).wait_send()


def panel_kernel(panel_hbm, mask_hbm, inv_hbm, tiles_hbm, root_hbm, factor_ref, rows_ref, cols_ref, root_ref,
                 panel_ref, mask_ref, given, tiles, prod, lent, slot_ref, got0, acc, coded, got, base, dmine, dsum, dgot, dpart, dparts, diag_ref,
                 state, inv_ref, load_sem, core_send, core_recv, send, recv, root_sem, dsend, drecv, *gather_sems):
    s, r, c = (lax.axis_index(a) for a in ("scen", "row", "col"))
    y, k = r // 2, lax.rem(r, 2)
    core = (s, 2 * y + 1 - k, c)
    x_to = (1 - s, r, c)
    y_to = (s, 2 * (1 - y) + k, c)
    par = lax.rem(c, 2)
    hi = c // 2
    z1 = (s, r, c + 1 - 2 * par)
    z2 = (s, r, lax.rem(c + 2, 4))
    me = s * 8 + y * 4 + c
    block = (s * 4 + r) * 8
    slots = tiles.shape[0]
    wide = root_ref.shape[1] // PANEL

    scalars = [
        pltpu.make_async_copy(panel_hbm, panel_ref, load_sem.at[0]),
        pltpu.make_async_copy(mask_hbm, mask_ref, load_sem.at[1]),
    ]
    loads = []
    for i in range(4):
        at = pl.ds(i * (slots // 4), slots // 4)
        loads.append(pltpu.make_async_copy(tiles_hbm.at[at], tiles.at[at], load_sem.at[2 + i]))
    for i in range(1):
        at = pl.ds(i * (given.shape[0] // 1), given.shape[0] // 1)
        loads.append(pltpu.make_async_copy(inv_hbm.at[at], given.at[at], load_sem.at[6 + i]))
    for cp in scalars + loads:
        cp.start()

    def chip(o):
        q = lax.rem(me + o, 16)
        return q, (q // 8, 2 * lax.rem(q // 4, 2) + k, lax.rem(q, 4))

    barrier = pltpu.get_barrier_semaphore()
    pl.semaphore_signal(barrier, inc=1, device_id=core, device_id_type=MESH_ID)
    for o in range(1, 16):
        pl.semaphore_signal(barrier, inc=1, device_id=chip(o)[1], device_id_type=MESH_ID)

    for cp in scalars:
        cp.wait()
    f = panel_ref[0]

    def place(t, at):
        flag = mask_ref[0, t]
        slot_ref[t] = jnp.where(flag == 1, at, slots)
        return at + flag

    lax.fori_loop(0, mask_ref.shape[1], place, 0)
    prod[slots] = jnp.zeros(prod.shape[1:], F32)
    for cp in loads[:4]:
        cp.wait()
    panel_slot = slot_ref[f]
    columns = tiles[jnp.minimum(panel_slot, slots - 1)]
    columns = jnp.where(panel_slot < slots, columns, jnp.zeros_like(columns))
    for cp in loads[4:]:
        cp.wait()
    root_copy = []
    for i in range(4):
        part = pl.ds(i * (root_ref.shape[0] // 4), root_ref.shape[0] // 4)
        cp = pltpu.make_async_copy(root_hbm.at[part], root_ref.at[part], root_sem.at[i])
        cp.start()
        root_copy.append(cp)
    weighted = lax.dot_general(
        columns, given[...], (((0,), (0,)), ((), ())), preferred_element_type=F32
    ).astype(BF16)
    for i in range(slots // 2):
        both = jnp.dot(
            weighted, jnp.concatenate([tiles[2 * i], tiles[2 * i + 1]], axis=1), preferred_element_type=F32
        )
        prod[2 * i] = both[:, :PANEL]
        prod[2 * i + 1] = both[:, PANEL:]

    pl.semaphore_wait(barrier, 16)
    order = ((1 - s) * 2 + 1 - y, (1 - s) * 2 + y, s * 2 + 1 - y, s * 2 + y)
    core_copy = []
    for n, i in enumerate(order):
        for t in range(8):
            lent[n, t] = prod[slot_ref[(i * 2 + 1 - k) * 8 + t]]
        cp = remote(lent.at[n], got0.at[n], core_send.at[n], core_recv.at[n], core)
        cp.start()
        core_copy.append(cp)

    pair = (2 * (1 - par), 2 * par)

    def core_sum(n, h, j):
        at = [4 * h + pair[j] + t for t in range(2)]
        return [prod[slot_ref[(order[n] * 2 + k) * 8 + a]] + got0[n, a] for a in at]

    def plus(a, b):
        return [a[t] + b[t] for t in range(2)]

    def ship(at, value, to):
        encode(value, coded.at[at])
        return remote(coded.at[at], got.at[at], send.at[at], recv.at[at], to)

    ways = (x_to, y_to)
    far, over, onward = ([[None, None], [None, None]] for _ in range(3))

    def far_send(j):
        for h in range(2):
            far[j][h] = ship(j * 2 + h, core_sum(0, h, j), ways[h])
            far[j][h].start()

    def over_make(j):
        for h in range(2):
            over[j][h] = ship(4 + j * 2 + h, core_sum(1 + h, h, j), ways[h])

    def onward_send(j):
        for h in range(2):
            far[j][h].wait_recv()
            value = plus(core_sum(2 - h, h, j), decode(got[j * 2 + h]))
            onward[j][h] = ship(8 + j * 2 + h, value, ways[1 - h])
            onward[j][h].start()

    def based(h, j):
        return plus(core_sum(3, h, j), [base[4 * h + pair[j] + t] for t in range(2)])

    def keep(j, h, value):
        for t in range(2):
            acc[j, h, t] = value[t]

    def kept(j, h):
        return [acc[j, h, t] for t in range(2)]

    core_copy[0].wait_recv()
    far_send(0)
    core_copy[1].wait_recv()
    core_copy[2].wait_recv()
    over_make(0)
    for h in range(2):
        over[0][h].start()
    far_send(1)
    over_make(1)

    for cp in root_copy:
        cp.wait()
    lane_block = lax.rem(f, wide)
    owner = c == f // wide

    def fetch_base(t, carry):
        at = pl.ds(pl.multiple_of(t * PANEL, PANEL), PANEL)
        value = jnp.zeros((PANEL, PANEL), F32)
        for j in range(wide):
            here = jnp.logical_and(owner, lane_block == j)
            value = jnp.where(here, root_ref[at, j * PANEL : (j + 1) * PANEL], value)
        base[t] = value.T
        return carry

    lax.fori_loop(0, 8, fetch_base, 0)
    own_diag = prod[slot_ref[f]]
    for t in range(8):
        own_diag = own_diag + jnp.where(block + t == f, base[t], 0.0)
    dmine[...] = own_diag
    core_diag = remote(dmine, dgot, dsend.at[0], drecv.at[0], core)
    core_diag.start()
    core_diag.wait()
    dsum[...] = dmine[...] + dgot[...]
    out1 = []
    for o in range(1, 16):
        q, dev = chip(o)
        cp = remote(dsum.at[pl.ds(pl.multiple_of(q * 8, 8), 8)], dparts.at[o], dsend.at[o], drecv.at[o], dev)
        cp.start()
        out1.append(cp)

    onward_send(0)
    for h in range(2):
        over[1][h].start()
    for cp in out1:
        cp.wait_recv()
    total = dsum[pl.ds(pl.multiple_of(me * 8, 8), 8), :]
    for o in range(1, 16):
        total = total + dparts[o]
    dpart[...] = total
    diag_ref[pl.ds(pl.multiple_of(me * 8, 8), 8), :] = total
    out2 = []
    for o in range(1, 16):
        q, dev = chip(o)
        cp = remote(dpart, diag_ref.at[pl.ds(pl.multiple_of(me * 8, 8), 8)], dsend.at[15 + o], drecv.at[15 + o], dev)
        cp.start()
        out2.append(cp)
    core_copy[3].wait_recv()
    for h in range(2):
        over[0][h].wait_recv()
        keep(0, h, plus(based(h, 0), decode(got[4 + h])))
        keep(1, h, based(h, 1))
    onward_send(1)
    z_out = []
    for h in range(2):
        onward[0][h].wait_recv()
        cp = ship(12 + h, plus(kept(0, h), decode(got[8 + h])), z1)
        cp.start()
        z_out.append(cp)
    for h in range(2):
        over[1][h].wait_recv()
        keep(1, h, plus(kept(1, h), decode(got[6 + h])))
    for h in range(2):
        onward[1][h].wait_recv()
        keep(1, h, plus(kept(1, h), decode(got[10 + h])))

    for h in range(2):
        z_out[h].wait_recv()
        cp = ship(14 + h, plus(kept(1, h), decode(got[12 + h])), z2)
        cp.start()
        z_out.append(cp)
    for cp in out2:
        cp.wait_recv()
    full = diag_ref[...]
    state[:, :PANEL] = 0.5 * (full + full.T)
    state[:, PANEL:] = jnp.where(
        lax.broadcasted_iota(jnp.int32, (PANEL, PANEL), 0) == lax.broadcasted_iota(jnp.int32, (PANEL, PANEL), 1),
        1.0, 0.0,
    )
    invert_blocks(state, inv_ref, 0, 8)

    inverse_parts = stack(thirds(inv_ref[...]), 1, 1)

    def solve(h):
        z_out[2 + h].wait_recv()
        mine, theirs = decode(coded[14 + h]), decode(got[14 + h])
        tiles_here = [block + 4 * h + 2 * par + t for t in range(2)]
        piece = jnp.concatenate(
            [jnp.where(tiles_here[t] == f, full, mine[t] + theirs[t]) for t in range(2)], axis=1
        )
        parts = lax.dot_general(
            stack(thirds(piece), 0, 0), inverse_parts, (((0,), (1,)), ((), ())), preferred_element_type=F32
        )
        for t in range(2):
            tile, part = tiles_here[t], parts[t * PANEL : (t + 1) * PANEL, :]

            @pl.when(hi == h)
            def _():
                factor_ref[t * PANEL : (t + 1) * PANEL, :] = jnp.where(tile >= f, part, 0.0)

            at = pl.ds(pl.multiple_of((4 * h + 2 * par + t) * PANEL, PANEL), PANEL)
            rows_ref[at, :] = jnp.where(tile > f, part, 0.0).astype(BF16)

    gather_phase(solve, rows_ref, cols_ref, *gather_sems)
    for cp in core_copy + out1 + out2 + far[0] + far[1] + over[0] + over[1] + onward[0] + onward[1] + z_out:
        cp.wait_send()


def panel_factor(panel_index, tile_mask, inverse, tiles, root_matrix):
    row_block, col_block = root_matrix.shape
    slots, inner, tile_rows = tiles.shape
    tile = (PANEL, tile_rows)
    hbm = pl.BlockSpec(memory_space=pltpu.HBM)
    vmem = pl.BlockSpec(memory_space=pltpu.VMEM)
    dma = pltpu.SemaphoreType.DMA
    return pl.pallas_call(
        panel_kernel,
        out_shape=(
            pltpu.VMEM((2 * PANEL, PANEL), F32),
            pltpu.VMEM((row_block, PANEL), BF16),
            pltpu.VMEM((col_block, PANEL), BF16),
            pltpu.VMEM((row_block, col_block), F32),
        ),
        in_specs=[hbm] * 5,
        out_specs=(vmem, vmem, vmem, vmem),
        scratch_shapes=[
            pltpu.SMEM((1,), jnp.int32),
            pltpu.SMEM(tile_mask.shape, jnp.int32),
            pltpu.VMEM(inverse.shape, BF16),
            pltpu.VMEM(tiles.shape, BF16),
            pltpu.VMEM((slots + 1, *tile), F32),
            pltpu.VMEM((4, 8, *tile), F32),
            pltpu.SMEM((tile_mask.shape[1],), jnp.int32),
            pltpu.VMEM((4, 8, *tile), F32),
            pltpu.VMEM((2, 2, 2, *tile), F32),
            pltpu.VMEM((16, CODED, PANEL), jnp.int16),
            pltpu.VMEM((16, CODED, PANEL), jnp.int16),
            pltpu.VMEM((8, *tile), F32),
            pltpu.VMEM(tile, F32),
            pltpu.VMEM(tile, F32),
            pltpu.VMEM(tile, F32),
            pltpu.VMEM((8, PANEL), F32),
            pltpu.VMEM((16, 8, PANEL), F32),
            pltpu.VMEM(tile, F32),
            pltpu.VMEM((PANEL, 2 * PANEL), F32),
            pltpu.VMEM(tile, F32),
            dma((7,)),
            dma((4,)),
            dma((4,)),
            dma((16,)),
            dma((16,)),
            dma((4,)),
            dma((31,)),
            dma((31,)),
            dma((2,)),
            dma((2,)),
            *[dma((4,))] * 5,
        ],
        compiler_params=pltpu.CompilerParams(collective_id=0, has_side_effects=True, vmem_limit_bytes=54 * 2**20),
        name="panel_factor",
    )(panel_index, tile_mask, inverse, tiles, root_matrix)


def trailing_kernel(root_ref, rows_ref, cols_ref, factor_ref, out_hbm, factor_hbm, held, sems):
    count = held.shape[0]
    rows = held.shape[1]
    copies = [pltpu.make_async_copy(factor_ref, factor_hbm, sems.at[count])]
    copies[0].start()
    for i in range(count):
        part = pl.ds(i * rows, rows)
        held[i] = root_ref[part, :] - lax.dot_general(
            rows_ref[part, :], cols_ref[...], (((1,), (1,)), ((), ())), preferred_element_type=F32
        )
        cp = pltpu.make_async_copy(held.at[i], out_hbm.at[part], sems.at[i])
        cp.start()
        copies.append(cp)
    for cp in copies:
        cp.wait()


def trailing_update(root, rows, cols, factor):
    hbm = pl.BlockSpec(memory_space=pltpu.HBM)
    vmem = pl.BlockSpec(memory_space=pltpu.VMEM)
    chunks = 8
    return pl.pallas_call(
        trailing_kernel,
        out_shape=(
            jax.ShapeDtypeStruct(root.shape, F32),
            jax.ShapeDtypeStruct(factor.shape, F32),
        ),
        in_specs=[vmem] * 4,
        out_specs=(hbm, hbm),
        scratch_shapes=[
            pltpu.VMEM((chunks, root.shape[0] // chunks, root.shape[1]), F32),
            pltpu.SemaphoreType.DMA((chunks + 1,)),
        ],
        compiler_params=pltpu.CompilerParams(vmem_limit_bytes=40 * 2**20),
        name="trailing_update",
    )(root, rows, cols, factor)


def direct(root_matrix, inverse_block, link_tiles, tile_mask, panel_index):
    factor, rows, cols, root = panel_factor(panel_index, tile_mask, inverse_block[0], link_tiles[0], root_matrix)
    return trailing_update(root, rows, cols, factor)


def solution(mesh):
    in_specs = (
        P(("scen", "row"), "col"),
        P(("scen", "row", "col"), None, None),
        P(("scen", "row", "col"), None, None, None),
        P(("scen", "row", "col"), None),
        P(),
    )
    out_specs = (P(("scen", "row"), "col"), P(("scen", "row", "col"), None))
    sizes = tuple(mesh.shape[a] for a in ("scen", "row", "col"))
    body = direct if sizes == (2, 4, 4) else local
    return jax.shard_map(body, mesh=mesh, in_specs=in_specs, out_specs=out_specs, check_vma=False)
```

```python
import jax
import jax.numpy as jnp
from jax import lax
from jax.experimental import pallas as pl
from jax.experimental.pallas import tpu as pltpu
from jax.sharding import PartitionSpec as P

PANEL = 128


def broadcast(block, axis, source):
    block = jnp.where(lax.axis_index(axis) == source, block, jnp.zeros_like(block))
    return lax.psum(block, axis)


def select_matrix(tile_flags, slot_count):
    tile_ids = jnp.arange(tile_flags.shape[0])
    slot_order = jnp.sum(jnp.where(tile_ids[None, :] <= tile_ids[:, None], tile_flags[None, :], 0), axis=1) - 1
    slot_ids = lax.broadcasted_iota(jnp.int32, (slot_count, tile_flags.shape[0]), 0)
    hit = (slot_order[None, :] == slot_ids) & (tile_flags[None, :] == 1)
    return jnp.where(hit, jnp.float32(1.0), jnp.float32(0.0))


def compact_term(inverse, tiles_here, tile_flags, panel_at):
    slot_count, inner_rows, tile_rows = tiles_here.shape
    selector = select_matrix(tile_flags, slot_count)
    per_panel = PANEL // tile_rows
    picked = lax.dynamic_slice_in_dim(selector, panel_at * per_panel, per_panel, 1)
    columns = jnp.einsum(
        "kj,knt->njt", picked.astype(jnp.bfloat16), tiles_here, preferred_element_type=jnp.float32
    )
    columns = columns.reshape(inner_rows, PANEL).astype(jnp.bfloat16)
    weighted = jnp.dot(inverse, columns, preferred_element_type=jnp.float32).astype(jnp.bfloat16)
    product = jnp.einsum("knt,na->kta", tiles_here, weighted, preferred_element_type=jnp.float32)
    return (selector, product)


def dense_term(selector, product, base_cols, base_start):
    spread = jnp.einsum("kr,kta->rta", selector, product, precision=lax.Precision.HIGHEST)
    scenario = spread.reshape(selector.shape[1] * product.shape[1], PANEL)
    own_block = lax.dynamic_slice_in_dim(scenario, base_start, base_cols.shape[0], 0) + base_cols
    return lax.dynamic_update_slice_in_dim(scenario, own_block, base_start, 0)


def lower_rows(diagonal, rows_here, first_row, first_col):
    chol_lower = jnp.linalg.cholesky(diagonal)
    solved = jax.scipy.linalg.solve_triangular(chol_lower, rows_here.T, lower=True).T
    row_ids = first_row + lax.broadcasted_iota(jnp.int32, (rows_here.shape[0], 1), 0)
    return jnp.where(row_ids >= first_col, solved, 0.0)


def trailing_rows(factor_part, first_row, first_col):
    rounded = factor_part.astype(jnp.bfloat16)
    row_ids = first_row + lax.broadcasted_iota(jnp.int32, (factor_part.shape[0], 1), 0)
    return jnp.where(row_ids >= first_col + PANEL, rounded, jnp.zeros_like(rounded))


def local(root_matrix, inverse_block, link_tiles, tile_mask, panel_index):
    panel_at = panel_index[0]
    tile_flags = tile_mask[0]
    selector, product = compact_term(inverse_block[0], link_tiles[0], tile_flags, panel_at)
    tile_count = selector.shape[1]
    tile_rows = product.shape[1]
    total_rows = tile_count * tile_rows
    row_block, col_block = root_matrix.shape
    scen_at = lax.axis_index("scen")
    row_at = lax.axis_index("row")
    col_at = lax.axis_index("col")
    row_count = lax.axis_size("row")
    col_count = lax.axis_size("col")
    scen_count = lax.axis_size("scen")
    block_at = scen_at * row_count + row_at
    first_col = panel_at * PANEL
    owner_col = first_col // col_block
    base_cols = lax.dynamic_slice_in_dim(root_matrix, first_col - owner_col * col_block, PANEL, 1)
    base_cols = jnp.where(col_at == owner_col, base_cols, 0.0)
    piece_rows = row_block // col_count
    scenario = dense_term(selector, product, base_cols, block_at * row_block)
    slab_rows = total_rows // scen_count
    slab_sum = lax.psum_scatter(scenario, "scen", scatter_dimension=0, tiled=True)
    slab_sum = lax.psum(slab_sum, ("row", "col"))
    owner_slab = first_col // slab_rows
    diag_part = lax.dynamic_slice_in_dim(slab_sum, first_col - owner_slab * slab_rows, PANEL, 0)
    diagonal = broadcast(diag_part, "scen", owner_slab)
    slab_first = scen_at * slab_rows
    slab_factor = lower_rows(diagonal, slab_sum, slab_first, first_col)
    factor_rows = lax.dynamic_slice_in_dim(
        slab_factor, (row_at * col_count + col_at) * piece_rows, piece_rows, 0
    )
    ending = trailing_rows(slab_factor, slab_first, first_col)
    all_factor = lax.all_gather(ending, "scen", axis=0, tiled=True)
    own_rows = lax.dynamic_slice_in_dim(all_factor, block_at * row_block, row_block, 0)
    own_cols = lax.dynamic_slice_in_dim(all_factor, col_at * col_block, col_block, 0)
    update = lax.dot_general(
        own_rows, own_cols, (((1,), (1,)), ((), ())), preferred_element_type=jnp.float32
    )
    return (root_matrix - update, factor_rows)


MESH_ID = pl.DeviceIdType.MESH
F32 = jnp.float32
BF16 = jnp.bfloat16


def remote(src, dst, send, recv, device):
    return pltpu.make_async_remote_copy(
        src_ref=src, dst_ref=dst, send_sem=send, recv_sem=recv, device_id=device, device_id_type=MESH_ID
    )


BLOCK = 16
CODED = 2 * PANEL + 16


def thirds(value):
    high = value.astype(BF16)
    rest = value - high.astype(F32)
    mid = rest.astype(BF16)
    return high, mid, (rest - mid.astype(F32)).astype(BF16)


TERMS = ((0, 0), (0, 1), (1, 0), (1, 1), (0, 2), (2, 0))


def stack(parts, side, axis):
    return jnp.concatenate([parts[term[side]] for term in TERMS], axis=axis)


def invert_blocks(state, inv_ref, start, stop):
    lane = lax.broadcasted_iota(jnp.int32, (BLOCK, PANEL), 1)
    sub = lax.broadcasted_iota(jnp.int32, (BLOCK, PANEL), 0)

    def block(b, carry):
        at = pl.ds(pl.multiple_of(b * BLOCK, BLOCK), BLOCK)
        left, right = state[at, :PANEL], state[at, PANEL:]
        cols = [
            jnp.broadcast_to(
                jnp.sum(jnp.where(lane == b * BLOCK + j, left, 0.0), axis=1, keepdims=True), (BLOCK, PANEL)
            )
            for j in range(BLOCK)
        ]
        for i in range(0, BLOCK, 2):
            first, cross, second = cols[i][i : i + 1, :], cols[i][i + 1 : i + 2, :], cols[i + 1][i + 1 : i + 2, :]
            det = first * second - cross * cross
            root_1, root_d = lax.rsqrt(first), lax.rsqrt(det)
            inv_1, inv_d = root_1 * root_1, root_d * root_d
            miss_1, miss_d = 1.0 - first * inv_1, 1.0 - det * inv_d
            root_1, inv_1 = root_1 + 0.5 * root_1 * miss_1, inv_1 + inv_1 * miss_1
            root_d, inv_d = root_d + 0.5 * root_d * miss_d, inv_d + inv_d * miss_d
            below_1 = jnp.where(sub > i + 1, cols[i], 0.0)
            below_2 = jnp.where(sub > i + 1, cols[i + 1], 0.0)
            coef_1 = (below_1 * second - below_2 * cross) * inv_d
            coef_2 = (below_2 * first - below_1 * cross) * inv_d
            for j in range(i + 2, BLOCK):
                cols[j] = cols[j] - (coef_1 * cols[j][i : i + 1, :] + coef_2 * cols[j][i + 1 : i + 2, :])
            root_2 = first * root_1 * root_d
            ratio = cross * inv_1

            def step(strip):
                row_1, row_2 = strip[i : i + 1, :], strip[i + 1 : i + 2, :]
                rest = strip - (coef_1 * row_1 + coef_2 * row_2)
                return jnp.where(
                    sub == i, row_1 * root_1, jnp.where(sub == i + 1, (row_2 - ratio * row_1) * root_2, rest)
                )

            left, right = step(left), step(right)
        inv_ref[at, :] = right
        later = thirds(jnp.where(lane >= b * BLOCK + BLOCK, left, 0.0))
        strip = thirds(jnp.concatenate([left, right], axis=1))
        state[...] = state[...] - lax.dot_general(
            stack(later, 0, 0), stack(strip, 1, 0), (((0,), (0,)), ((), ())), preferred_element_type=F32
        )
        return carry

    lax.fori_loop(start, stop, block, 0)


def code_scale(exponent):
    return jnp.exp2(15.0 - exponent) * 0.995


def encode(pair, out):
    exps = []
    for t in range(2):
        top = jnp.max(jnp.abs(pair[t]), axis=0, keepdims=True)
        exponent = jnp.ceil(jnp.log2(jnp.maximum(top, 1e-30)))
        out[t * PANEL : (t + 1) * PANEL, :] = jnp.round(pair[t] * code_scale(exponent)).astype(jnp.int32).astype(jnp.int16)
        exps.append(jnp.broadcast_to(exponent, (8, PANEL)))
    out[2 * PANEL : CODED, :] = jnp.concatenate(exps, axis=0).astype(jnp.int32).astype(jnp.int16)


def decode(coded):
    exponent = coded[2 * PANEL : CODED, :].astype(jnp.int32).astype(F32)
    return [
        coded[t * PANEL : (t + 1) * PANEL, :].astype(jnp.int32).astype(F32)
        * (1.0 / code_scale(exponent[8 * t : 8 * t + 1, :]))
        for t in range(2)
    ]


def gather_phase(solve, drain, rows_ref, cols_ref, send_z, recv_z, send_x, send_y, recv_p, send_c, recv_c):
    s, r, c = (lax.axis_index(a) for a in ("scen", "row", "col"))
    y, k = r // 2, lax.rem(r, 2)
    rows = 2 * PANEL
    far_x = lax.rem(s + c // 2, 2)
    far_y = lax.rem(y + c, 2)
    source = jnp.logical_and(far_x == 0, far_y == 0)
    beside_x = jnp.logical_and(far_x == 1, far_y == 0)
    beside_y = jnp.logical_and(far_x == 0, far_y == 1)
    across = jnp.logical_and(far_x == 1, far_y == 1)
    x_to = (1 - s, r, c)
    y_to = (s, 2 * (1 - y) + k, c)
    core = (s, 2 * y + 1 - k, c)
    par = lax.rem(c, 2)
    pieces = (par, par + 2, 1 - par, 3 - par)

    def row_at(z):
        return rows_ref.at[pl.ds(pl.multiple_of(z * rows, rows), rows)]

    def col_at(kk, z):
        return cols_ref.at[pl.ds(pl.multiple_of((kk * 4 + z) * rows, rows), rows)]

    middle = jnp.logical_or(c == 1, c == 2)

    def z_copy(i, way):
        to = (s, r, 3 - c) if way == 0 else (s, r, jnp.where(c == 1, 0, 3))
        return remote(row_at(pieces[i]), row_at(pieces[i]), send_z.at[2 * way + i], recv_z.at[i], to)

    def z_arrival(i):
        return remote(row_at(pieces[2 + i]), row_at(pieces[2 + i]), send_z.at[i], recv_z.at[i], core)

    def first_hop(o, to, sems):
        return remote(row_at(pieces[o]), col_at(k, pieces[o]), sems.at[o], recv_p.at[o], to)

    def onward(o):
        here = col_at(k, pieces[o])
        return remote(here, here, (send_x if o % 2 else send_y).at[o], recv_p.at[o], x_to if o % 2 else y_to)

    def forwards(o):
        if o % 2:
            return jnp.logical_and(far_x == 0, far_y == 1)
        return jnp.logical_and(far_x == 1, far_y == 0)

    def to_core_first(o):
        remote(row_at(pieces[o]), col_at(k, pieces[o]), send_c.at[o], recv_c.at[o], core).start()

    def to_core(o, kk):
        here = col_at(kk, pieces[o])
        return remote(here, here, send_c.at[o], recv_c.at[o], core)

    def finish(o):
        onward(o).wait_recv()

        @pl.when(forwards(o))
        def _():
            onward(o).start()

        to_core(o, k).start()

    for o in range(2):
        solve(o)

        @pl.when(source)
        def _():
            if o == 0:
                first_hop(0, x_to, send_x).start()
            else:
                first_hop(1, y_to, send_y).start()
            to_core_first(o)

        @pl.when(middle)
        def _():
            z_copy(o, 0).start()
            z_copy(o, 1).start()

    drain()

    @pl.when(source)
    def _():
        z_arrival(0).wait_recv()
        first_hop(2, x_to, send_x).start()
        z_arrival(1).wait_recv()
        first_hop(3, y_to, send_y).start()
        for o in range(2, 4):
            to_core_first(o)
        for o in range(4):
            col_at(k, pieces[o])[...] = row_at(pieces[o])[...]
        for o in (1, 3):
            first_hop(o, x_to, send_x).start()
        for o in (0, 2):
            first_hop(o, y_to, send_y).start()

    for place, turn in ((beside_x, (0, 2, 1, 3)), (beside_y, (1, 3, 0, 2)), (across, (0, 1, 2, 3))):

        @pl.when(place)
        def _():
            for o in turn:
                finish(o)

    @pl.when(jnp.logical_not(source))
    def _():
        for i in range(2):
            z_arrival(i).wait_recv()

    for o in range(4):
        to_core(o, 1 - k).wait_recv()
        to_core(o, k).wait_send()

        @pl.when(source)
        def _():
            first_hop(o, x_to, send_x).wait_send()
            first_hop(o, y_to, send_y).wait_send()

        @pl.when(forwards(o))
        def _():
            onward(o).wait_send()

    @pl.when(middle)
    def _():
        for i in range(2):
            z_copy(i, 0).wait_send()
            z_copy(i, 1).wait_send()


def panel_kernel(panel_hbm, mask_hbm, inv_hbm, tiles_hbm, root_hbm, factor_ref, rows_ref, cols_ref, root_ref,
                 panel_ref, mask_ref, given, tiles, prod, lent, slot_ref, got0, acc, coded, got, base, dmine, dsum, dgot, dpart, dparts, diag_ref,
                 state, inv_ref, load_sem, core_send, core_recv, send, recv, root_sem, dsend, drecv, *gather_sems):
    s, r, c = (lax.axis_index(a) for a in ("scen", "row", "col"))
    y, k = r // 2, lax.rem(r, 2)
    core = (s, 2 * y + 1 - k, c)
    x_to = (1 - s, r, c)
    y_to = (s, 2 * (1 - y) + k, c)
    par = lax.rem(c, 2)
    hi = c // 2
    z1 = (s, r, c + 1 - 2 * par)
    z2 = (s, r, lax.rem(c + 2, 4))
    me = s * 8 + y * 4 + c
    block = (s * 4 + r) * 8
    slots = tiles.shape[0]
    wide = root_ref.shape[1] // PANEL

    scalars = [
        pltpu.make_async_copy(panel_hbm, panel_ref, load_sem.at[0]),
        pltpu.make_async_copy(mask_hbm, mask_ref, load_sem.at[1]),
    ]
    loads = []
    for i in range(4):
        at = pl.ds(i * (slots // 4), slots // 4)
        loads.append(pltpu.make_async_copy(tiles_hbm.at[at], tiles.at[at], load_sem.at[2 + i]))
    for i in range(1):
        at = pl.ds(i * (given.shape[0] // 1), given.shape[0] // 1)
        loads.append(pltpu.make_async_copy(inv_hbm.at[at], given.at[at], load_sem.at[6 + i]))
    for cp in scalars + loads:
        cp.start()

    def chip(o):
        q = lax.rem(me + o, 16)
        return q, (q // 8, 2 * lax.rem(q // 4, 2) + k, lax.rem(q, 4))

    barrier = pltpu.get_barrier_semaphore()
    pl.semaphore_signal(barrier, inc=1, device_id=core, device_id_type=MESH_ID)
    for o in range(1, 16):
        pl.semaphore_signal(barrier, inc=1, device_id=chip(o)[1], device_id_type=MESH_ID)

    for cp in scalars:
        cp.wait()
    f = panel_ref[0]

    def place(t, at):
        flag = mask_ref[0, t]
        slot_ref[t] = jnp.where(flag == 1, at, slots)
        return at + flag

    lax.fori_loop(0, mask_ref.shape[1], place, 0)
    prod[slots] = jnp.zeros(prod.shape[1:], F32)
    for cp in loads[:4]:
        cp.wait()
    panel_slot = slot_ref[f]
    columns = tiles[jnp.minimum(panel_slot, slots - 1)]
    columns = jnp.where(panel_slot < slots, columns, jnp.zeros_like(columns))
    for cp in loads[4:]:
        cp.wait()
    root_copy = []
    for i in range(4):
        part = pl.ds(i * (root_ref.shape[0] // 4), root_ref.shape[0] // 4)
        cp = pltpu.make_async_copy(root_hbm.at[part], root_ref.at[part], root_sem.at[i])
        cp.start()
        root_copy.append(cp)
    weighted = lax.dot_general(
        columns, given[...], (((0,), (0,)), ((), ())), preferred_element_type=F32
    ).astype(BF16)
    for i in range(slots // 2):
        both = jnp.dot(
            weighted, jnp.concatenate([tiles[2 * i], tiles[2 * i + 1]], axis=1), preferred_element_type=F32
        )
        prod[2 * i] = both[:, :PANEL]
        prod[2 * i + 1] = both[:, PANEL:]

    pl.semaphore_wait(barrier, 16)
    order = ((1 - s) * 2 + 1 - y, (1 - s) * 2 + y, s * 2 + 1 - y, s * 2 + y)
    core_copy = []
    for n, i in enumerate(order):
        for t in range(8):
            lent[n, t] = prod[slot_ref[(i * 2 + 1 - k) * 8 + t]]
        cp = remote(lent.at[n], got0.at[n], core_send.at[n], core_recv.at[n], core)
        cp.start()
        core_copy.append(cp)

    pair = (2 * (1 - par), 2 * par)

    def core_sum(n, h, j):
        at = [4 * h + pair[j] + t for t in range(2)]
        return [prod[slot_ref[(order[n] * 2 + k) * 8 + a]] + got0[n, a] for a in at]

    def plus(a, b):
        return [a[t] + b[t] for t in range(2)]

    def ship(at, value, to):
        encode(value, coded.at[at])
        return remote(coded.at[at], got.at[at], send.at[at], recv.at[at], to)

    ways = (x_to, y_to)
    far, over, onward = ([[None, None], [None, None]] for _ in range(3))

    def far_send(j):
        for h in range(2):
            far[j][h] = ship(j * 2 + h, core_sum(0, h, j), ways[h])
            far[j][h].start()

    def over_make(j):
        for h in range(2):
            over[j][h] = ship(4 + j * 2 + h, core_sum(1 + h, h, j), ways[h])

    def onward_send(j):
        for h in range(2):
            far[j][h].wait_recv()
            value = plus(core_sum(2 - h, h, j), decode(got[j * 2 + h]))
            onward[j][h] = ship(8 + j * 2 + h, value, ways[1 - h])
            onward[j][h].start()

    def based(h, j):
        return plus(core_sum(3, h, j), [base[4 * h + pair[j] + t] for t in range(2)])

    def keep(j, h, value):
        for t in range(2):
            acc[j, h, t] = value[t]

    def kept(j, h):
        return [acc[j, h, t] for t in range(2)]

    core_copy[0].wait_recv()
    far_send(0)
    core_copy[1].wait_recv()
    core_copy[2].wait_recv()
    over_make(0)
    for h in range(2):
        over[0][h].start()
    far_send(1)
    over_make(1)

    for cp in root_copy:
        cp.wait()
    lane_block = lax.rem(f, wide)
    owner = c == f // wide

    def fetch_base(t, carry):
        at = pl.ds(pl.multiple_of(t * PANEL, PANEL), PANEL)
        value = jnp.zeros((PANEL, PANEL), F32)
        for j in range(wide):
            here = jnp.logical_and(owner, lane_block == j)
            value = jnp.where(here, root_ref[at, j * PANEL : (j + 1) * PANEL], value)
        base[t] = value.T
        return carry

    lax.fori_loop(0, 8, fetch_base, 0)
    own_diag = prod[slot_ref[f]]
    for t in range(8):
        own_diag = own_diag + jnp.where(block + t == f, base[t], 0.0)
    dmine[...] = own_diag
    core_diag = remote(dmine, dgot, dsend.at[0], drecv.at[0], core)
    core_diag.start()
    core_diag.wait()
    dsum[...] = dmine[...] + dgot[...]
    out1 = []
    for o in range(1, 16):
        q, dev = chip(o)
        cp = remote(dsum.at[pl.ds(pl.multiple_of(q * 8, 8), 8)], dparts.at[o], dsend.at[o], drecv.at[o], dev)
        cp.start()
        out1.append(cp)

    onward_send(0)
    for h in range(2):
        over[1][h].start()
    for cp in out1:
        cp.wait_recv()
    total = dsum[pl.ds(pl.multiple_of(me * 8, 8), 8), :]
    for o in range(1, 16):
        total = total + dparts[o]
    dpart[...] = total
    diag_ref[pl.ds(pl.multiple_of(me * 8, 8), 8), :] = total
    out2 = []
    for o in range(1, 16):
        q, dev = chip(o)
        cp = remote(dpart, diag_ref.at[pl.ds(pl.multiple_of(me * 8, 8), 8)], dsend.at[15 + o], drecv.at[15 + o], dev)
        cp.start()
        out2.append(cp)
    core_copy[3].wait_recv()
    for h in range(2):
        over[0][h].wait_recv()
        keep(0, h, plus(based(h, 0), decode(got[4 + h])))
        keep(1, h, based(h, 1))
    onward_send(1)
    z_out = []
    for h in range(2):
        onward[0][h].wait_recv()
        cp = ship(12 + h, plus(kept(0, h), decode(got[8 + h])), z1)
        cp.start()
        z_out.append(cp)
    for h in range(2):
        over[1][h].wait_recv()
        keep(1, h, plus(kept(1, h), decode(got[6 + h])))
    for h in range(2):
        onward[1][h].wait_recv()
        keep(1, h, plus(kept(1, h), decode(got[10 + h])))

    for h in range(2):
        z_out[h].wait_recv()
        cp = ship(14 + h, plus(kept(1, h), decode(got[12 + h])), z2)
        cp.start()
        z_out.append(cp)
    for cp in out2:
        cp.wait_recv()
    full = diag_ref[...]
    state[:, :PANEL] = 0.5 * (full + full.T)
    state[:, PANEL:] = jnp.where(
        lax.broadcasted_iota(jnp.int32, (PANEL, PANEL), 0) == lax.broadcasted_iota(jnp.int32, (PANEL, PANEL), 1),
        1.0, 0.0,
    )
    invert_blocks(state, inv_ref, 0, 8)

    inverse_parts = stack(thirds(inv_ref[...]), 1, 1)

    def solve(h):
        z_out[2 + h].wait_recv()
        mine, theirs = decode(coded[14 + h]), decode(got[14 + h])
        tiles_here = [block + 4 * h + 2 * par + t for t in range(2)]
        piece = jnp.concatenate(
            [jnp.where(tiles_here[t] == f, full, mine[t] + theirs[t]) for t in range(2)], axis=1
        )
        parts = lax.dot_general(
            stack(thirds(piece), 0, 0), inverse_parts, (((0,), (1,)), ((), ())), preferred_element_type=F32
        )
        for t in range(2):
            tile, part = tiles_here[t], parts[t * PANEL : (t + 1) * PANEL, :]

            @pl.when(hi == h)
            def _():
                factor_ref[t * PANEL : (t + 1) * PANEL, :] = jnp.where(tile >= f, part, 0.0)

            at = pl.ds(pl.multiple_of((4 * h + 2 * par + t) * PANEL, PANEL), PANEL)
            rows_ref[at, :] = jnp.where(tile > f, part, 0.0).astype(BF16)

    def drain():
        for cp in core_copy + out1 + out2 + far[0] + far[1] + over[0] + over[1] + onward[0] + onward[1] + z_out:
            cp.wait_send()

    gather_phase(solve, drain, rows_ref, cols_ref, *gather_sems)


def panel_factor(panel_index, tile_mask, inverse, tiles, root_matrix):
    row_block, col_block = root_matrix.shape
    slots, inner, tile_rows = tiles.shape
    tile = (PANEL, tile_rows)
    hbm = pl.BlockSpec(memory_space=pltpu.HBM)
    vmem = pl.BlockSpec(memory_space=pltpu.VMEM)
    dma = pltpu.SemaphoreType.DMA
    return pl.pallas_call(
        panel_kernel,
        out_shape=(
            pltpu.VMEM((2 * PANEL, PANEL), F32),
            pltpu.VMEM((row_block, PANEL), BF16),
            pltpu.VMEM((col_block, PANEL), BF16),
            pltpu.VMEM((row_block, col_block), F32),
        ),
        in_specs=[hbm] * 5,
        out_specs=(vmem, vmem, vmem, vmem),
        scratch_shapes=[
            pltpu.SMEM((1,), jnp.int32),
            pltpu.SMEM(tile_mask.shape, jnp.int32),
            pltpu.VMEM(inverse.shape, BF16),
            pltpu.VMEM(tiles.shape, BF16),
            pltpu.VMEM((slots + 1, *tile), F32),
            pltpu.VMEM((4, 8, *tile), F32),
            pltpu.SMEM((tile_mask.shape[1],), jnp.int32),
            pltpu.VMEM((4, 8, *tile), F32),
            pltpu.VMEM((2, 2, 2, *tile), F32),
            pltpu.VMEM((16, CODED, PANEL), jnp.int16),
            pltpu.VMEM((16, CODED, PANEL), jnp.int16),
            pltpu.VMEM((8, *tile), F32),
            pltpu.VMEM(tile, F32),
            pltpu.VMEM(tile, F32),
            pltpu.VMEM(tile, F32),
            pltpu.VMEM((8, PANEL), F32),
            pltpu.VMEM((16, 8, PANEL), F32),
            pltpu.VMEM(tile, F32),
            pltpu.VMEM((PANEL, 2 * PANEL), F32),
            pltpu.VMEM(tile, F32),
            dma((7,)),
            dma((4,)),
            dma((4,)),
            dma((16,)),
            dma((16,)),
            dma((4,)),
            dma((31,)),
            dma((31,)),
            dma((4,)),
            dma((2,)),
            *[dma((4,))] * 5,
        ],
        compiler_params=pltpu.CompilerParams(collective_id=0, has_side_effects=True, vmem_limit_bytes=54 * 2**20),
        name="panel_factor",
    )(panel_index, tile_mask, inverse, tiles, root_matrix)


def trailing_kernel(root_ref, rows_ref, cols_ref, factor_ref, out_hbm, factor_hbm, held, sems):
    count = held.shape[0]
    rows = held.shape[1]
    copies = [pltpu.make_async_copy(factor_ref, factor_hbm, sems.at[count])]
    copies[0].start()
    for i in range(count):
        part = pl.ds(i * rows, rows)
        held[i] = root_ref[part, :] - lax.dot_general(
            rows_ref[part, :], cols_ref[...], (((1,), (1,)), ((), ())), preferred_element_type=F32
        )
        cp = pltpu.make_async_copy(held.at[i], out_hbm.at[part], sems.at[i])
        cp.start()
        copies.append(cp)
    for cp in copies:
        cp.wait()


def trailing_update(root, rows, cols, factor):
    hbm = pl.BlockSpec(memory_space=pltpu.HBM)
    vmem = pl.BlockSpec(memory_space=pltpu.VMEM)
    chunks = 8
    return pl.pallas_call(
        trailing_kernel,
        out_shape=(
            jax.ShapeDtypeStruct(root.shape, F32),
            jax.ShapeDtypeStruct(factor.shape, F32),
        ),
        in_specs=[vmem] * 4,
        out_specs=(hbm, hbm),
        scratch_shapes=[
            pltpu.VMEM((chunks, root.shape[0] // chunks, root.shape[1]), F32),
            pltpu.SemaphoreType.DMA((chunks + 1,)),
        ],
        compiler_params=pltpu.CompilerParams(vmem_limit_bytes=40 * 2**20),
        name="trailing_update",
    )(root, rows, cols, factor)


def direct(root_matrix, inverse_block, link_tiles, tile_mask, panel_index):
    factor, rows, cols, root = panel_factor(panel_index, tile_mask, inverse_block[0], link_tiles[0], root_matrix)
    return trailing_update(root, rows, cols, factor)


def solution(mesh):
    in_specs = (
        P(("scen", "row"), "col"),
        P(("scen", "row", "col"), None, None),
        P(("scen", "row", "col"), None, None, None),
        P(("scen", "row", "col"), None),
        P(),
    )
    out_specs = (P(("scen", "row"), "col"), P(("scen", "row", "col"), None))
    sizes = tuple(mesh.shape[a] for a in ("scen", "row", "col"))
    body = direct if sizes == (2, 4, 4) else local
    return jax.shard_map(body, mesh=mesh, in_specs=in_specs, out_specs=out_specs, check_vma=False)
```

```python
import jax
import jax.numpy as jnp
from jax import lax
from jax.experimental import pallas as pl
from jax.experimental.pallas import tpu as pltpu
from jax.sharding import PartitionSpec as P

PANEL = 128


def broadcast(block, axis, source):
    block = jnp.where(lax.axis_index(axis) == source, block, jnp.zeros_like(block))
    return lax.psum(block, axis)


def select_matrix(tile_flags, slot_count):
    tile_ids = jnp.arange(tile_flags.shape[0])
    slot_order = jnp.sum(jnp.where(tile_ids[None, :] <= tile_ids[:, None], tile_flags[None, :], 0), axis=1) - 1
    slot_ids = lax.broadcasted_iota(jnp.int32, (slot_count, tile_flags.shape[0]), 0)
    hit = (slot_order[None, :] == slot_ids) & (tile_flags[None, :] == 1)
    return jnp.where(hit, jnp.float32(1.0), jnp.float32(0.0))


def compact_term(inverse, tiles_here, tile_flags, panel_at):
    slot_count, inner_rows, tile_rows = tiles_here.shape
    selector = select_matrix(tile_flags, slot_count)
    per_panel = PANEL // tile_rows
    picked = lax.dynamic_slice_in_dim(selector, panel_at * per_panel, per_panel, 1)
    columns = jnp.einsum(
        "kj,knt->njt", picked.astype(jnp.bfloat16), tiles_here, preferred_element_type=jnp.float32
    )
    columns = columns.reshape(inner_rows, PANEL).astype(jnp.bfloat16)
    weighted = jnp.dot(inverse, columns, preferred_element_type=jnp.float32).astype(jnp.bfloat16)
    product = jnp.einsum("knt,na->kta", tiles_here, weighted, preferred_element_type=jnp.float32)
    return (selector, product)


def dense_term(selector, product, base_cols, base_start):
    spread = jnp.einsum("kr,kta->rta", selector, product, precision=lax.Precision.HIGHEST)
    scenario = spread.reshape(selector.shape[1] * product.shape[1], PANEL)
    own_block = lax.dynamic_slice_in_dim(scenario, base_start, base_cols.shape[0], 0) + base_cols
    return lax.dynamic_update_slice_in_dim(scenario, own_block, base_start, 0)


def lower_rows(diagonal, rows_here, first_row, first_col):
    chol_lower = jnp.linalg.cholesky(diagonal)
    solved = jax.scipy.linalg.solve_triangular(chol_lower, rows_here.T, lower=True).T
    row_ids = first_row + lax.broadcasted_iota(jnp.int32, (rows_here.shape[0], 1), 0)
    return jnp.where(row_ids >= first_col, solved, 0.0)


def trailing_rows(factor_part, first_row, first_col):
    rounded = factor_part.astype(jnp.bfloat16)
    row_ids = first_row + lax.broadcasted_iota(jnp.int32, (factor_part.shape[0], 1), 0)
    return jnp.where(row_ids >= first_col + PANEL, rounded, jnp.zeros_like(rounded))


def local(root_matrix, inverse_block, link_tiles, tile_mask, panel_index):
    panel_at = panel_index[0]
    tile_flags = tile_mask[0]
    selector, product = compact_term(inverse_block[0], link_tiles[0], tile_flags, panel_at)
    tile_count = selector.shape[1]
    tile_rows = product.shape[1]
    total_rows = tile_count * tile_rows
    row_block, col_block = root_matrix.shape
    scen_at = lax.axis_index("scen")
    row_at = lax.axis_index("row")
    col_at = lax.axis_index("col")
    row_count = lax.axis_size("row")
    col_count = lax.axis_size("col")
    scen_count = lax.axis_size("scen")
    block_at = scen_at * row_count + row_at
    first_col = panel_at * PANEL
    owner_col = first_col // col_block
    base_cols = lax.dynamic_slice_in_dim(root_matrix, first_col - owner_col * col_block, PANEL, 1)
    base_cols = jnp.where(col_at == owner_col, base_cols, 0.0)
    piece_rows = row_block // col_count
    scenario = dense_term(selector, product, base_cols, block_at * row_block)
    slab_rows = total_rows // scen_count
    slab_sum = lax.psum_scatter(scenario, "scen", scatter_dimension=0, tiled=True)
    slab_sum = lax.psum(slab_sum, ("row", "col"))
    owner_slab = first_col // slab_rows
    diag_part = lax.dynamic_slice_in_dim(slab_sum, first_col - owner_slab * slab_rows, PANEL, 0)
    diagonal = broadcast(diag_part, "scen", owner_slab)
    slab_first = scen_at * slab_rows
    slab_factor = lower_rows(diagonal, slab_sum, slab_first, first_col)
    factor_rows = lax.dynamic_slice_in_dim(
        slab_factor, (row_at * col_count + col_at) * piece_rows, piece_rows, 0
    )
    ending = trailing_rows(slab_factor, slab_first, first_col)
    all_factor = lax.all_gather(ending, "scen", axis=0, tiled=True)
    own_rows = lax.dynamic_slice_in_dim(all_factor, block_at * row_block, row_block, 0)
    own_cols = lax.dynamic_slice_in_dim(all_factor, col_at * col_block, col_block, 0)
    update = lax.dot_general(
        own_rows, own_cols, (((1,), (1,)), ((), ())), preferred_element_type=jnp.float32
    )
    return (root_matrix - update, factor_rows)


MESH_ID = pl.DeviceIdType.MESH
F32 = jnp.float32
BF16 = jnp.bfloat16


def remote(src, dst, send, recv, device):
    return pltpu.make_async_remote_copy(
        src_ref=src, dst_ref=dst, send_sem=send, recv_sem=recv, device_id=device, device_id_type=MESH_ID
    )


BLOCK = 16
CODED = 2 * PANEL + 16


def thirds(value):
    high = value.astype(BF16)
    rest = value - high.astype(F32)
    mid = rest.astype(BF16)
    return high, mid, (rest - mid.astype(F32)).astype(BF16)


TERMS = ((0, 0), (0, 1), (1, 0), (1, 1), (0, 2), (2, 0))


def stack(parts, side, axis):
    return jnp.concatenate([parts[term[side]] for term in TERMS], axis=axis)


def invert_blocks(state, inv_ref, start, stop):
    lane = lax.broadcasted_iota(jnp.int32, (BLOCK, PANEL), 1)
    sub = lax.broadcasted_iota(jnp.int32, (BLOCK, PANEL), 0)

    def block(b, carry):
        at = pl.ds(pl.multiple_of(b * BLOCK, BLOCK), BLOCK)
        left, right = state[at, :PANEL], state[at, PANEL:]
        cols = [
            jnp.broadcast_to(
                jnp.sum(jnp.where(lane == b * BLOCK + j, left, 0.0), axis=1, keepdims=True), (BLOCK, PANEL)
            )
            for j in range(BLOCK)
        ]
        for i in range(0, BLOCK, 2):
            first, cross, second = cols[i][i : i + 1, :], cols[i][i + 1 : i + 2, :], cols[i + 1][i + 1 : i + 2, :]
            det = first * second - cross * cross
            root_1, root_d = lax.rsqrt(first), lax.rsqrt(det)
            inv_1, inv_d = root_1 * root_1, root_d * root_d
            miss_1, miss_d = 1.0 - first * inv_1, 1.0 - det * inv_d
            root_1, inv_1 = root_1 + 0.5 * root_1 * miss_1, inv_1 + inv_1 * miss_1
            root_d, inv_d = root_d + 0.5 * root_d * miss_d, inv_d + inv_d * miss_d
            below_1 = jnp.where(sub > i + 1, cols[i], 0.0)
            below_2 = jnp.where(sub > i + 1, cols[i + 1], 0.0)
            coef_1 = (below_1 * second - below_2 * cross) * inv_d
            coef_2 = (below_2 * first - below_1 * cross) * inv_d
            for j in range(i + 2, BLOCK):
                cols[j] = cols[j] - (coef_1 * cols[j][i : i + 1, :] + coef_2 * cols[j][i + 1 : i + 2, :])
            root_2 = first * root_1 * root_d
            ratio = cross * inv_1

            def step(strip):
                row_1, row_2 = strip[i : i + 1, :], strip[i + 1 : i + 2, :]
                rest = strip - (coef_1 * row_1 + coef_2 * row_2)
                return jnp.where(
                    sub == i, row_1 * root_1, jnp.where(sub == i + 1, (row_2 - ratio * row_1) * root_2, rest)
                )

            left, right = step(left), step(right)
        inv_ref[at, :] = right
        later = thirds(jnp.where(lane >= b * BLOCK + BLOCK, left, 0.0))
        strip = thirds(jnp.concatenate([left, right], axis=1))
        state[...] = state[...] - lax.dot_general(
            stack(later, 0, 0), stack(strip, 1, 0), (((0,), (0,)), ((), ())), preferred_element_type=F32
        )
        return carry

    lax.fori_loop(start, stop, block, 0)


def code_scale(exponent):
    return jnp.exp2(15.0 - exponent) * 0.995


def encode(pair, out):
    exps = []
    for t in range(2):
        top = jnp.max(jnp.abs(pair[t]), axis=0, keepdims=True)
        exponent = jnp.ceil(jnp.log2(jnp.maximum(top, 1e-30)))
        out[t * PANEL : (t + 1) * PANEL, :] = jnp.round(pair[t] * code_scale(exponent)).astype(jnp.int32).astype(jnp.int16)
        exps.append(jnp.broadcast_to(exponent, (8, PANEL)))
    out[2 * PANEL : CODED, :] = jnp.concatenate(exps, axis=0).astype(jnp.int32).astype(jnp.int16)


def decode(coded):
    exponent = coded[2 * PANEL : CODED, :].astype(jnp.int32).astype(F32)
    return [
        coded[t * PANEL : (t + 1) * PANEL, :].astype(jnp.int32).astype(F32)
        * (1.0 / code_scale(exponent[8 * t : 8 * t + 1, :]))
        for t in range(2)
    ]


def gather_phase(solve, drain, rows_ref, cols_ref, send_z, recv_z, send_x, send_y, recv_p, send_c, recv_c):
    s, r, c = (lax.axis_index(a) for a in ("scen", "row", "col"))
    y, k = r // 2, lax.rem(r, 2)
    rows = 2 * PANEL
    far_x = lax.rem(s + c // 2, 2)
    far_y = lax.rem(y + c, 2)
    source = jnp.logical_and(far_x == 0, far_y == 0)
    beside_x = jnp.logical_and(far_x == 1, far_y == 0)
    beside_y = jnp.logical_and(far_x == 0, far_y == 1)
    across = jnp.logical_and(far_x == 1, far_y == 1)
    x_to = (1 - s, r, c)
    y_to = (s, 2 * (1 - y) + k, c)
    core = (s, 2 * y + 1 - k, c)
    par = lax.rem(c, 2)
    pieces = (par, par + 2, 1 - par, 3 - par)

    def row_at(z):
        return rows_ref.at[pl.ds(pl.multiple_of(z * rows, rows), rows)]

    def col_at(kk, z):
        return cols_ref.at[pl.ds(pl.multiple_of((kk * 4 + z) * rows, rows), rows)]

    middle = jnp.logical_or(c == 1, c == 2)

    def z_copy(i, way):
        to = (s, r, 3 - c) if way == 0 else (s, r, jnp.where(c == 1, 0, 3))
        return remote(row_at(pieces[i]), row_at(pieces[i]), send_z.at[2 * way + i], recv_z.at[i], to)

    def z_arrival(i):
        return remote(row_at(pieces[2 + i]), row_at(pieces[2 + i]), send_z.at[i], recv_z.at[i], core)

    def first_hop(o, to, sems):
        return remote(row_at(pieces[o]), col_at(k, pieces[o]), sems.at[o], recv_p.at[o], to)

    def onward(o):
        here = col_at(k, pieces[o])
        return remote(here, here, (send_x if o % 2 else send_y).at[o], recv_p.at[o], x_to if o % 2 else y_to)

    def forwards(o):
        if o % 2:
            return jnp.logical_and(far_x == 0, far_y == 1)
        return jnp.logical_and(far_x == 1, far_y == 0)

    def to_core_first(o):
        remote(row_at(pieces[o]), col_at(k, pieces[o]), send_c.at[o], recv_c.at[o], core).start()

    def to_core(o, kk):
        here = col_at(kk, pieces[o])
        return remote(here, here, send_c.at[o], recv_c.at[o], core)

    def finish(o):
        onward(o).wait_recv()

        @pl.when(forwards(o))
        def _():
            onward(o).start()

        to_core(o, k).start()

    for o in range(2):
        solve(o)

        @pl.when(source)
        def _():
            if o == 0:
                first_hop(0, x_to, send_x).start()
            else:
                first_hop(1, y_to, send_y).start()
            to_core_first(o)

        @pl.when(middle)
        def _():
            z_copy(o, 1).start()
            z_copy(o, 0).start()

    drain()

    @pl.when(source)
    def _():
        z_arrival(0).wait_recv()
        first_hop(2, x_to, send_x).start()
        z_arrival(1).wait_recv()
        first_hop(3, y_to, send_y).start()
        for o in range(2, 4):
            to_core_first(o)
        for o in range(4):
            col_at(k, pieces[o])[...] = row_at(pieces[o])[...]
        for o in (1, 3):
            first_hop(o, x_to, send_x).start()
        for o in (0, 2):
            first_hop(o, y_to, send_y).start()

    for place, turn in ((beside_x, (0, 2, 1, 3)), (beside_y, (1, 3, 0, 2)), (across, (0, 1, 2, 3))):

        @pl.when(place)
        def _():
            for o in turn:
                finish(o)

    @pl.when(jnp.logical_not(source))
    def _():
        for i in range(2):
            z_arrival(i).wait_recv()

    for o in range(4):
        to_core(o, 1 - k).wait_recv()
        to_core(o, k).wait_send()

        @pl.when(source)
        def _():
            first_hop(o, x_to, send_x).wait_send()
            first_hop(o, y_to, send_y).wait_send()

        @pl.when(forwards(o))
        def _():
            onward(o).wait_send()

    @pl.when(middle)
    def _():
        for i in range(2):
            z_copy(i, 0).wait_send()
            z_copy(i, 1).wait_send()


def panel_kernel(panel_hbm, mask_hbm, inv_hbm, tiles_hbm, root_hbm, factor_ref, rows_ref, cols_ref, root_ref,
                 panel_ref, mask_ref, given, tiles, prod, lent, slot_ref, got0, acc, coded, got, base, dmine, dsum, dgot, dpart, dparts, diag_ref,
                 state, inv_ref, load_sem, core_send, core_recv, send, recv, root_sem, dsend, drecv, *gather_sems):
    s, r, c = (lax.axis_index(a) for a in ("scen", "row", "col"))
    y, k = r // 2, lax.rem(r, 2)
    core = (s, 2 * y + 1 - k, c)
    x_to = (1 - s, r, c)
    y_to = (s, 2 * (1 - y) + k, c)
    par = lax.rem(c, 2)
    hi = c // 2
    z1 = (s, r, c + 1 - 2 * par)
    z2 = (s, r, lax.rem(c + 2, 4))
    me = s * 8 + y * 4 + c
    block = (s * 4 + r) * 8
    slots = tiles.shape[0]
    wide = root_ref.shape[1] // PANEL

    scalars = [
        pltpu.make_async_copy(panel_hbm, panel_ref, load_sem.at[0]),
        pltpu.make_async_copy(mask_hbm, mask_ref, load_sem.at[1]),
    ]
    loads = []
    for i in range(4):
        at = pl.ds(i * (slots // 4), slots // 4)
        loads.append(pltpu.make_async_copy(tiles_hbm.at[at], tiles.at[at], load_sem.at[2 + i]))
    for i in range(1):
        at = pl.ds(i * (given.shape[0] // 1), given.shape[0] // 1)
        loads.append(pltpu.make_async_copy(inv_hbm.at[at], given.at[at], load_sem.at[6 + i]))
    for cp in scalars + loads:
        cp.start()

    def chip(o):
        q = lax.rem(me + o, 16)
        return q, (q // 8, 2 * lax.rem(q // 4, 2) + k, lax.rem(q, 4))

    barrier = pltpu.get_barrier_semaphore()
    pl.semaphore_signal(barrier, inc=1, device_id=core, device_id_type=MESH_ID)
    for o in range(1, 16):
        pl.semaphore_signal(barrier, inc=1, device_id=chip(o)[1], device_id_type=MESH_ID)

    for cp in scalars:
        cp.wait()
    f = panel_ref[0]

    def place(t, at):
        flag = mask_ref[0, t]
        slot_ref[t] = jnp.where(flag == 1, at, slots)
        return at + flag

    lax.fori_loop(0, mask_ref.shape[1], place, 0)
    prod[slots] = jnp.zeros(prod.shape[1:], F32)
    for cp in loads[:4]:
        cp.wait()
    panel_slot = slot_ref[f]
    columns = tiles[jnp.minimum(panel_slot, slots - 1)]
    columns = jnp.where(panel_slot < slots, columns, jnp.zeros_like(columns))
    for cp in loads[4:]:
        cp.wait()
    root_copy = []
    for i in range(4):
        part = pl.ds(i * (root_ref.shape[0] // 4), root_ref.shape[0] // 4)
        cp = pltpu.make_async_copy(root_hbm.at[part], root_ref.at[part], root_sem.at[i])
        cp.start()
        root_copy.append(cp)
    weighted = lax.dot_general(
        columns, given[...], (((0,), (0,)), ((), ())), preferred_element_type=F32
    ).astype(BF16)
    for i in range(slots // 2):
        both = jnp.dot(
            weighted, jnp.concatenate([tiles[2 * i], tiles[2 * i + 1]], axis=1), preferred_element_type=F32
        )
        prod[2 * i] = both[:, :PANEL]
        prod[2 * i + 1] = both[:, PANEL:]

    pl.semaphore_wait(barrier, 16)
    order = ((1 - s) * 2 + 1 - y, (1 - s) * 2 + y, s * 2 + 1 - y, s * 2 + y)
    core_copy = []
    for n, i in enumerate(order):
        for t in range(8):
            lent[n, t] = prod[slot_ref[(i * 2 + 1 - k) * 8 + t]]
        cp = remote(lent.at[n], got0.at[n], core_send.at[n], core_recv.at[n], core)
        cp.start()
        core_copy.append(cp)

    pair = (2 * (1 - par), 2 * par)

    def core_sum(n, h, j):
        at = [4 * h + pair[j] + t for t in range(2)]
        return [prod[slot_ref[(order[n] * 2 + k) * 8 + a]] + got0[n, a] for a in at]

    def plus(a, b):
        return [a[t] + b[t] for t in range(2)]

    def ship(at, value, to):
        encode(value, coded.at[at])
        return remote(coded.at[at], got.at[at], send.at[at], recv.at[at], to)

    ways = (x_to, y_to)
    far, over, onward = ([[None, None], [None, None]] for _ in range(3))

    def far_send(j):
        for h in range(2):
            far[j][h] = ship(j * 2 + h, core_sum(0, h, j), ways[h])
            far[j][h].start()

    def over_make(j):
        for h in range(2):
            over[j][h] = ship(4 + j * 2 + h, core_sum(1 + h, h, j), ways[h])

    def onward_send(j):
        for h in range(2):
            far[j][h].wait_recv()
            value = plus(core_sum(2 - h, h, j), decode(got[j * 2 + h]))
            onward[j][h] = ship(8 + j * 2 + h, value, ways[1 - h])
            onward[j][h].start()

    def based(h, j):
        return plus(core_sum(3, h, j), [base[4 * h + pair[j] + t] for t in range(2)])

    def keep(j, h, value):
        for t in range(2):
            acc[j, h, t] = value[t]

    def kept(j, h):
        return [acc[j, h, t] for t in range(2)]

    core_copy[0].wait_recv()
    far_send(0)
    core_copy[1].wait_recv()
    core_copy[2].wait_recv()
    over_make(0)
    for h in range(2):
        over[0][h].start()
    far_send(1)
    over_make(1)

    for cp in root_copy:
        cp.wait()
    lane_block = lax.rem(f, wide)
    owner = c == f // wide

    def fetch_base(t, carry):
        at = pl.ds(pl.multiple_of(t * PANEL, PANEL), PANEL)
        value = jnp.zeros((PANEL, PANEL), F32)
        for j in range(wide):
            here = jnp.logical_and(owner, lane_block == j)
            value = jnp.where(here, root_ref[at, j * PANEL : (j + 1) * PANEL], value)
        base[t] = value.T
        return carry

    lax.fori_loop(0, 8, fetch_base, 0)
    own_diag = prod[slot_ref[f]]
    for t in range(8):
        own_diag = own_diag + jnp.where(block + t == f, base[t], 0.0)
    dmine[...] = own_diag
    core_diag = remote(dmine, dgot, dsend.at[0], drecv.at[0], core)
    core_diag.start()
    core_diag.wait()
    dsum[...] = dmine[...] + dgot[...]
    out1 = []
    for o in range(1, 16):
        q, dev = chip(o)
        cp = remote(dsum.at[pl.ds(pl.multiple_of(q * 8, 8), 8)], dparts.at[o], dsend.at[o], drecv.at[o], dev)
        cp.start()
        out1.append(cp)

    onward_send(0)
    for h in range(2):
        over[1][h].start()
    for cp in out1:
        cp.wait_recv()
    total = dsum[pl.ds(pl.multiple_of(me * 8, 8), 8), :]
    for o in range(1, 16):
        total = total + dparts[o]
    dpart[...] = total
    diag_ref[pl.ds(pl.multiple_of(me * 8, 8), 8), :] = total
    out2 = []
    for o in range(1, 16):
        q, dev = chip(o)
        cp = remote(dpart, diag_ref.at[pl.ds(pl.multiple_of(me * 8, 8), 8)], dsend.at[15 + o], drecv.at[15 + o], dev)
        cp.start()
        out2.append(cp)
    core_copy[3].wait_recv()
    for h in range(2):
        over[0][h].wait_recv()
        keep(0, h, plus(based(h, 0), decode(got[4 + h])))
        keep(1, h, based(h, 1))
    onward_send(1)
    z_out = []
    for h in range(2):
        onward[0][h].wait_recv()
        cp = ship(12 + h, plus(kept(0, h), decode(got[8 + h])), z1)
        cp.start()
        z_out.append(cp)
    for h in range(2):
        over[1][h].wait_recv()
        keep(1, h, plus(kept(1, h), decode(got[6 + h])))
    for h in range(2):
        onward[1][h].wait_recv()
        keep(1, h, plus(kept(1, h), decode(got[10 + h])))

    for h in range(2):
        z_out[h].wait_recv()
        cp = ship(14 + h, plus(kept(1, h), decode(got[12 + h])), z2)
        cp.start()
        z_out.append(cp)
    for cp in out2:
        cp.wait_recv()
    full = diag_ref[...]
    state[:, :PANEL] = 0.5 * (full + full.T)
    state[:, PANEL:] = jnp.where(
        lax.broadcasted_iota(jnp.int32, (PANEL, PANEL), 0) == lax.broadcasted_iota(jnp.int32, (PANEL, PANEL), 1),
        1.0, 0.0,
    )
    invert_blocks(state, inv_ref, 0, 8)

    inverse_parts = stack(thirds(inv_ref[...]), 1, 1)

    def solve(h):
        z_out[2 + h].wait_recv()
        mine, theirs = decode(coded[14 + h]), decode(got[14 + h])
        tiles_here = [block + 4 * h + 2 * par + t for t in range(2)]
        piece = jnp.concatenate(
            [jnp.where(tiles_here[t] == f, full, mine[t] + theirs[t]) for t in range(2)], axis=1
        )
        parts = lax.dot_general(
            stack(thirds(piece), 0, 0), inverse_parts, (((0,), (1,)), ((), ())), preferred_element_type=F32
        )
        for t in range(2):
            tile, part = tiles_here[t], parts[t * PANEL : (t + 1) * PANEL, :]

            @pl.when(hi == h)
            def _():
                factor_ref[t * PANEL : (t + 1) * PANEL, :] = jnp.where(tile >= f, part, 0.0)

            at = pl.ds(pl.multiple_of((4 * h + 2 * par + t) * PANEL, PANEL), PANEL)
            rows_ref[at, :] = jnp.where(tile > f, part, 0.0).astype(BF16)

    def drain():
        for cp in core_copy + out1 + out2 + far[0] + far[1] + over[0] + over[1] + onward[0] + onward[1] + z_out:
            cp.wait_send()

    gather_phase(solve, drain, rows_ref, cols_ref, *gather_sems)


def panel_factor(panel_index, tile_mask, inverse, tiles, root_matrix):
    row_block, col_block = root_matrix.shape
    slots, inner, tile_rows = tiles.shape
    tile = (PANEL, tile_rows)
    hbm = pl.BlockSpec(memory_space=pltpu.HBM)
    vmem = pl.BlockSpec(memory_space=pltpu.VMEM)
    dma = pltpu.SemaphoreType.DMA
    return pl.pallas_call(
        panel_kernel,
        out_shape=(
            pltpu.VMEM((2 * PANEL, PANEL), F32),
            pltpu.VMEM((row_block, PANEL), BF16),
            pltpu.VMEM((col_block, PANEL), BF16),
            pltpu.VMEM((row_block, col_block), F32),
        ),
        in_specs=[hbm] * 5,
        out_specs=(vmem, vmem, vmem, vmem),
        scratch_shapes=[
            pltpu.SMEM((1,), jnp.int32),
            pltpu.SMEM(tile_mask.shape, jnp.int32),
            pltpu.VMEM(inverse.shape, BF16),
            pltpu.VMEM(tiles.shape, BF16),
            pltpu.VMEM((slots + 1, *tile), F32),
            pltpu.VMEM((4, 8, *tile), F32),
            pltpu.SMEM((tile_mask.shape[1],), jnp.int32),
            pltpu.VMEM((4, 8, *tile), F32),
            pltpu.VMEM((2, 2, 2, *tile), F32),
            pltpu.VMEM((16, CODED, PANEL), jnp.int16),
            pltpu.VMEM((16, CODED, PANEL), jnp.int16),
            pltpu.VMEM((8, *tile), F32),
            pltpu.VMEM(tile, F32),
            pltpu.VMEM(tile, F32),
            pltpu.VMEM(tile, F32),
            pltpu.VMEM((8, PANEL), F32),
            pltpu.VMEM((16, 8, PANEL), F32),
            pltpu.VMEM(tile, F32),
            pltpu.VMEM((PANEL, 2 * PANEL), F32),
            pltpu.VMEM(tile, F32),
            dma((7,)),
            dma((4,)),
            dma((4,)),
            dma((16,)),
            dma((16,)),
            dma((4,)),
            dma((31,)),
            dma((31,)),
            dma((4,)),
            dma((2,)),
            *[dma((4,))] * 5,
        ],
        compiler_params=pltpu.CompilerParams(collective_id=0, has_side_effects=True, vmem_limit_bytes=54 * 2**20),
        name="panel_factor",
    )(panel_index, tile_mask, inverse, tiles, root_matrix)


def trailing_kernel(root_ref, rows_ref, cols_ref, factor_ref, out_hbm, factor_hbm, held, sems):
    count = held.shape[0]
    rows = held.shape[1]
    copies = [pltpu.make_async_copy(factor_ref, factor_hbm, sems.at[count])]
    copies[0].start()
    for i in range(count):
        part = pl.ds(i * rows, rows)
        held[i] = root_ref[part, :] - lax.dot_general(
            rows_ref[part, :], cols_ref[...], (((1,), (1,)), ((), ())), preferred_element_type=F32
        )
        cp = pltpu.make_async_copy(held.at[i], out_hbm.at[part], sems.at[i])
        cp.start()
        copies.append(cp)
    for cp in copies:
        cp.wait()


def trailing_update(root, rows, cols, factor):
    hbm = pl.BlockSpec(memory_space=pltpu.HBM)
    vmem = pl.BlockSpec(memory_space=pltpu.VMEM)
    chunks = 8
    return pl.pallas_call(
        trailing_kernel,
        out_shape=(
            jax.ShapeDtypeStruct(root.shape, F32),
            jax.ShapeDtypeStruct(factor.shape, F32),
        ),
        in_specs=[vmem] * 4,
        out_specs=(hbm, hbm),
        scratch_shapes=[
            pltpu.VMEM((chunks, root.shape[0] // chunks, root.shape[1]), F32),
            pltpu.SemaphoreType.DMA((chunks + 1,)),
        ],
        compiler_params=pltpu.CompilerParams(vmem_limit_bytes=40 * 2**20),
        name="trailing_update",
    )(root, rows, cols, factor)


def direct(root_matrix, inverse_block, link_tiles, tile_mask, panel_index):
    factor, rows, cols, root = panel_factor(panel_index, tile_mask, inverse_block[0], link_tiles[0], root_matrix)
    return trailing_update(root, rows, cols, factor)


def solution(mesh):
    in_specs = (
        P(("scen", "row"), "col"),
        P(("scen", "row", "col"), None, None),
        P(("scen", "row", "col"), None, None, None),
        P(("scen", "row", "col"), None),
        P(),
    )
    out_specs = (P(("scen", "row"), "col"), P(("scen", "row", "col"), None))
    sizes = tuple(mesh.shape[a] for a in ("scen", "row", "col"))
    body = direct if sizes == (2, 4, 4) else local
    return jax.shard_map(body, mesh=mesh, in_specs=in_specs, out_specs=out_specs, check_vma=False)
```
